256 devices in a mesh: depth: 16 (over z, y_lo), freq: 16 (over y_hi, x, core).
Axes of the slice: x: 4, y: 4 (y_hi: 2, y_lo: 2; y = y_hi * 2 + y_lo), z: 8, core: 2. Of those that a mesh axis runs over, the one named last changes fastest.
Arguments:
- extrap: bfloat16 [16, 16, 2, 1024, 1024], P('depth', 'freq'), may hold values from -0.125 to 0.125
- source_field: bfloat16 [16, 128, 2, 1024], P('freq'), may hold values from -6 to 6
- record_field: bfloat16 [16, 128, 2, 1024], P('freq'), may hold values from -6 to 6
- shot_of_record: int32 [128], replicated, may hold values from 0 to 127, each once
- freq_index: int32 [16], P('freq'), may hold values from 0 to 127, as said below
- angle_lag: int32 [1024, 256], replicated, may hold values from 0 to 15
Outputs:
- gathers: float32 [1024, 16, 256], P(('freq', 'depth'))
The draws below stay inside these ranges and needn't reach their ends.
Inputs may be any that keep to these rules, and one draw needn't show every extreme that they name: `shot_of_record`: each shot is named once. `freq_index`: the frequency numbers are distinct, and the largest one, 127, is always held by some slot.
All inputs are finite; a program needn't handle non-finite values.
Results may differ from the reference program's by a relative error of at most 0.035.
Values may be sent and summed in bfloat16 or wider, within the bound.
A program may use at most 64 MiB of HBM per device.

```python
import math
import jax
import jax.numpy as jnp
from jax import lax

X = 1024
ANGLES = 256
SHOTS = 128
NZ = 16
FREQS = 16


def draw_freq_index(key, part):
    others = jax.random.permutation(jax.random.fold_in(key, 11), 8 * FREQS - 1)[:FREQS - 1]
    values = jnp.concatenate([others.astype(jnp.int32), jnp.full((1,), 8 * FREQS - 1, jnp.int32)])
    order = jax.random.permutation(jax.random.fold_in(key, 12), FREQS)
    return values[order].astype(jnp.int32)


def touch_ends(drawn, rng, smallest, top_value):
    spot = [jax.random.randint(jax.random.fold_in(rng, axis), (), 0, length) for axis, length in enumerate(drawn.shape)]
    widest = drawn.shape.index(max(drawn.shape))
    beside = spot[:widest] + [(spot[widest] + 1) % drawn.shape[widest]] + spot[widest + 1:]
    return drawn.at[tuple(spot)].set(smallest).at[tuple(beside)].set(top_value)


def levels(rng, shape, split, smallest, high):
    def one(dim, blocks):
        heights = jax.random.uniform(jax.random.fold_in(jax.random.fold_in(rng, 6), dim), (blocks,), jnp.float32, smallest / len(split), high / len(split))
        return jnp.repeat(jnp.exp(heights), shape[dim] // blocks).reshape((-1,) + (1,) * (len(shape) - dim - 1))

    loudness = one(*split[0])
    for cut in split[1:]:
        loudness = loudness * one(*cut)
    return loudness


def noise(rng, shape, width, reach, shards=(), held_as=jnp.bfloat16):
    values = width * jax.random.normal(rng, shape, jnp.float32)
    if shards:
        values = values * levels(rng, shape, shards, -0.22, 0.18)
    return jnp.clip(values, -reach, reach).astype(held_as)


def setup_inputs(seed: int = 0) -> dict:
    keys = jax.random.split(jax.random.key(seed), 7)
    extrap = noise(keys[0], (NZ, FREQS, 2, X, X), (2 * X) ** -0.5, 0.125, ((0, 16), (1, 16)))
    source_field = noise(keys[1], (FREQS, SHOTS, 2, X), 1.0, 6.0, ((0, 16),))
    record_field = noise(keys[2], (FREQS, SHOTS, 2, X), 1.0, 6.0, ((0, 16),))
    shot_of_record = jax.random.permutation(keys[3], SHOTS).astype(jnp.int32)
    freq_index = draw_freq_index(jax.random.fold_in(keys[6], 71), 0)
    angle_lag = touch_ends(jax.random.randint(keys[5], (X, ANGLES), 0, NZ), jax.random.fold_in(keys[5], 1), 0, NZ - 1).astype(jnp.int32)
    return dict(extrap=extrap, source_field=source_field, record_field=record_field, shot_of_record=shot_of_record, freq_index=freq_index, angle_lag=angle_lag)


def make_block(real_part, imag_part):
    upper = jnp.concatenate([real_part, imag_part], axis=1)
    lower = jnp.concatenate([-imag_part, real_part], axis=1)
    return jnp.concatenate([upper, lower], axis=0)

def reference(extrap, source_field, record_field, shot_of_record, freq_index, angle_lag):
    points = source_field.shape[3]
    shot_count = source_field.shape[1]
    weights = (freq_index.astype(jnp.float32) + 1.0) / (8 * FREQS)
    factor = 1.0 / math.sqrt(SHOTS * FREQS)
    paired = source_field[:, shot_of_record].reshape(FREQS, shot_count, 2 * points)
    records = jnp.concatenate([record_field[:, :, 1], record_field[:, :, 0]], axis=2)
    source_list = [paired[freq_slot] for freq_slot in range(FREQS)]
    record_list = [records[freq_slot] for freq_slot in range(FREQS)]
    image_list = []
    for depth_level in range(NZ):
        image = jnp.zeros((points, points), jnp.float32)
        for freq_slot in range(FREQS):
            extrapolator = make_block(extrap[depth_level, freq_slot, 0], extrap[depth_level, freq_slot, 1])
            stacked = jnp.concatenate([source_list[freq_slot], record_list[freq_slot]], axis=0)
            advanced = jnp.dot(stacked, extrapolator, preferred_element_type=jnp.float32).astype(jnp.bfloat16)
            source_list[freq_slot] = advanced[:shot_count]
            record_list[freq_slot] = advanced[shot_count:]
            source_stack = advanced[:shot_count].reshape(2 * shot_count, points)
            record_stack = advanced[shot_count:].reshape(shot_count, 2, points)[:, ::-1].reshape(2 * shot_count, points)
            partial_value = lax.dot_general(source_stack, record_stack, (((0,), (0,)), ((), ())), preferred_element_type=jnp.float32)
            image = image + partial_value * (weights[freq_slot] * factor)
        image_list.append(image.astype(jnp.bfloat16))
    images = jnp.stack(image_list, axis=0)
    padded = jnp.concatenate([images, jnp.zeros_like(images)], axis=0)
    stacked_sum = jnp.zeros((points * NZ, ANGLES), jnp.float32)
    for lag_value in range(NZ):
        shifted = jnp.transpose(padded[lag_value:lag_value + NZ], (1, 0, 2)).reshape(points * NZ, points)
        selector = (angle_lag == lag_value).astype(jnp.bfloat16)
        stacked_sum = stacked_sum + jnp.dot(shifted, selector, preferred_element_type=jnp.float32)
    return (stacked_sum / math.sqrt(points)).reshape(points, NZ, ANGLES)
```

```python
import math

import jax
import jax.numpy as jnp
from jax import lax
from jax.experimental import pallas as pl
from jax.experimental.pallas import tpu as pltpu
from jax.sharding import PartitionSpec as P

MESH = pl.DeviceIdType.MESH
BATCH = 8


def chain_kernel(depth_count, batch_count, e_ref, x_ref, out_ref, inbuf, send_sem, recv_sem):
    d = lax.axis_index("depth")
    barrier = pltpu.get_barrier_semaphore()

    @pl.when(d > 0)
    def _():
        pl.semaphore_signal(barrier, inc=1, device_id={"depth": d - 1}, device_id_type=MESH)

    @pl.when(d < depth_count - 1)
    def _():
        pl.semaphore_wait(barrier, 1)

    @pl.when(d == 0)
    def _():
        inbuf[...] = x_ref[...]

    half = 2 * BATCH

    def hop(b):
        rows = pl.ds(pl.multiple_of(b * half, half), half)
        return pltpu.make_async_remote_copy(
            src_ref=out_ref.at[:, rows, :],
            dst_ref=inbuf.at[:, rows, :],
            send_sem=send_sem.at[b],
            recv_sem=recv_sem.at[b],
            device_id={"depth": d + 1},
            device_id_type=MESH,
        )

    def step(b, carry):
        rows = pl.ds(pl.multiple_of(b * half, half), half)

        @pl.when(d > 0)
        def _():
            hop(b).wait_recv()

        values = inbuf[:, rows, :].reshape(2 * half, -1)
        first = jnp.dot(values, e_ref[0], preferred_element_type=jnp.float32)
        second = jnp.dot(values, e_ref[1], preferred_element_type=jnp.float32)
        m = BATCH
        source = jnp.concatenate(
            [first[:m] - second[m : 2 * m], second[:m] + first[m : 2 * m]], axis=0
        )
        record = jnp.concatenate(
            [first[2 * m : 3 * m] + second[3 * m :], first[3 * m :] - second[2 * m : 3 * m]], axis=0
        )
        out_ref[0, rows, :] = source.astype(jnp.bfloat16)
        out_ref[1, rows, :] = record.astype(jnp.bfloat16)

        @pl.when(d < depth_count - 1)
        def _():
            hop(b).start()

        return carry

    lax.fori_loop(0, batch_count, step, 0)

    @pl.when(d < depth_count - 1)
    def _():
        def drain(b, carry):
            hop(b).wait_send()
            return carry

        lax.fori_loop(0, batch_count, drain, 0)


def run_chain(extrap, packed, depth_count):
    rows = packed.shape[1]
    points = packed.shape[2]
    batch_count = rows // (2 * BATCH)

    def body(*refs):
        chain_kernel(depth_count, batch_count, *refs)

    return pl.pallas_call(
        body,
        out_shape=jax.ShapeDtypeStruct(packed.shape, jnp.bfloat16),
        in_specs=[pl.BlockSpec(memory_space=pltpu.VMEM)] * 2,
        out_specs=pl.BlockSpec(memory_space=pltpu.VMEM),
        scratch_shapes=[
            pltpu.VMEM((2, rows, points), jnp.bfloat16),
            pltpu.SemaphoreType.DMA((batch_count,)),
            pltpu.SemaphoreType.DMA((batch_count,)),
        ],
        compiler_params=pltpu.CompilerParams(
            collective_id=0, has_side_effects=True, vmem_limit_bytes=32 * 1024 * 1024
        ),
        name="chain",
    )(extrap, packed)


def shards(extrap, source_field, record_field, shot_of_record, freq_index, angle_lag):
    depth_count = lax.axis_size("depth")
    freq_count = lax.axis_size("freq")
    points = source_field.shape[3]
    shot_count = source_field.shape[1]
    paired = jnp.take(source_field[0], shot_of_record, axis=0)

    def pack(field):
        split = field.reshape(shot_count // BATCH, BATCH, 2, points)
        return split.transpose(0, 2, 1, 3).reshape(2 * shot_count, points)

    packed = jnp.stack([pack(paired), pack(record_field[0])])
    finished = run_chain(extrap[0, 0], packed, depth_count)
    factor = (
        (freq_index[0].astype(jnp.float32) + 1.0)
        / (8 * freq_count)
        / math.sqrt(shot_count * freq_count)
    )
    partial_value = lax.dot_general(
        finished[0], finished[1], (((0,), (0,)), ((), ())), preferred_element_type=jnp.float32
    )
    image_panel = lax.psum_scatter(
        (partial_value * factor).astype(jnp.bfloat16), "freq", scatter_dimension=0, tiled=True
    )
    gathered = lax.all_to_all(
        image_panel[:, None, :], "depth", split_axis=0, concat_axis=1, tiled=True
    )
    row_count = gathered.shape[0]
    padded = jnp.concatenate([gathered, jnp.zeros_like(gathered)], axis=1)

    def add_lagged(lag_value, stacked_sum):
        shifted = lax.dynamic_slice_in_dim(padded, lag_value, depth_count, 1).reshape(
            row_count * depth_count, points
        )
        selector = (angle_lag == lag_value).astype(jnp.bfloat16)
        return stacked_sum + jnp.dot(shifted, selector, preferred_element_type=jnp.float32)

    stacked_sum = lax.fori_loop(
        0,
        depth_count,
        add_lagged,
        jnp.zeros((row_count * depth_count, angle_lag.shape[1]), jnp.float32),
    )
    return (stacked_sum / math.sqrt(points)).reshape(row_count, depth_count, angle_lag.shape[1])


def solution(mesh):
    placed = (
        P("depth", "freq", None, None, None),
        P("freq", None, None, None),
        P("freq", None, None, None),
        P(),
        P("freq"),
        P(),
    )
    return jax.shard_map(
        shards,
        mesh=mesh,
        in_specs=placed,
        out_specs=P(("freq", "depth"), None, None),
        check_vma=False,
    )
```

```python
import math

import jax
import jax.numpy as jnp
from jax import lax
from jax.experimental import pallas as pl
from jax.experimental.pallas import tpu as pltpu
from jax.sharding import PartitionSpec as P

MESH = pl.DeviceIdType.MESH
BATCH = 8
DEPTHS = 16
ROWS = 64
POINTS = 1024
ANGLES = 256
SHOTS = 128
LANES = 128
BATCHES = SHOTS // BATCH
HALF = 2 * BATCH
PIECE = ROWS // DEPTHS
ORDER = [(1, 2), (1, 1), (1, 3), (1, 0), (0, 2), (0, 1), (0, 3), (0, 0)]
F32 = jnp.float32
BF16 = jnp.bfloat16


def kernel(
    e_hbm, x_ref, factor_ref, lag_ref, out_ref,
    e_ref, inbuf, fin, sel, part, corein, two, one, three, rel_up, rel_down, from_down, from_up,
    ysend, yin, acc, pieces, gath, xs, g,
    e_sem, chain_send, chain_recv, core_send, core_recv, x_send, x_recv, y_send, y_recv, d_send, d_recv,
):
    d = lax.axis_index("depth")
    f = lax.axis_index("freq")
    core = f % 2
    x = (f // 2) % 4
    yh = f // 8
    partner = f + 1 - 2 * core
    up = yh * 8 + ((x + 1) % 4) * 2 + core
    down = yh * 8 + ((x + 3) % 4) * 2 + core
    across = f + 8 - 16 * yh

    load_e = pltpu.make_async_copy(e_hbm, e_ref, e_sem)
    load_e.start()
    barrier = pltpu.get_barrier_semaphore()
    for other in (partner, up, down, across):
        pl.semaphore_signal(barrier, inc=1, device_id={"freq": other}, device_id_type=MESH)

    def greet(k, carry):
        pl.semaphore_signal(
            barrier, inc=1, device_id={"depth": (d + k) % DEPTHS}, device_id_type=MESH
        )
        return carry

    lax.fori_loop(1, DEPTHS, greet, 0)

    def build():
        def one_lag(lag, carry):
            sel[lag] = jnp.where(lag_ref[...] == lag, 1.0, 0.0).astype(BF16)
            g[lag, :, ROWS:, :] = jnp.zeros((2, ROWS, LANES), F32)
            return carry

        lax.fori_loop(0, DEPTHS, one_lag, 0)

    @pl.when(d > 0)
    def _():
        build()

    @pl.when(d == 0)
    def _():
        inbuf[...] = x_ref[...]

    load_e.wait()
    pl.semaphore_wait(barrier, 4 + DEPTHS - 1)

    def hop(b):
        rows = pl.ds(pl.multiple_of(b * HALF, HALF), HALF)
        return pltpu.make_async_remote_copy(
            src_ref=fin.at[:, rows, :],
            dst_ref=inbuf.at[:, rows, :],
            send_sem=chain_send.at[b],
            recv_sem=chain_recv.at[b],
            device_id={"depth": d + 1},
            device_id_type=MESH,
        )

    def step(b, carry):
        rows = pl.ds(pl.multiple_of(b * HALF, HALF), HALF)

        @pl.when(d > 0)
        def _():
            hop(b).wait_recv()

        values = inbuf[:, rows, :].reshape(2 * HALF, POINTS)
        first = jnp.dot(values, e_ref[0], preferred_element_type=F32)
        second = jnp.dot(values, e_ref[1], preferred_element_type=F32)
        m = BATCH
        source = jnp.concatenate(
            [first[:m] - second[m : 2 * m], second[:m] + first[m : 2 * m]], axis=0
        )
        record = jnp.concatenate(
            [first[2 * m : 3 * m] + second[3 * m :], first[3 * m :] - second[2 * m : 3 * m]], axis=0
        )
        fin[0, rows, :] = source.astype(BF16)
        fin[1, rows, :] = record.astype(BF16)

        @pl.when(d < DEPTHS - 1)
        def _():
            hop(b).start()

        return carry

    lax.fori_loop(0, BATCHES, step, 0)

    mine = pl.ds(pl.multiple_of(core * ROWS, ROWS), ROWS)
    theirs = pl.ds(pl.multiple_of((1 - core) * ROWS, ROWS), ROWS)

    def to_core(t):
        return pltpu.make_async_remote_copy(
            src_ref=part.at[t, theirs, :],
            dst_ref=corein.at[t],
            send_sem=core_send.at[t],
            recv_sem=core_recv.at[t],
            device_id={"freq": partner},
            device_id_type=MESH,
        )

    factor = factor_ref[0]
    for t, (q, r) in enumerate(ORDER):
        block = (yh + q * (1 - 2 * yh)) * 4 + (x + r) % 4
        columns = pl.ds(pl.multiple_of(block * 2 * ROWS, 2 * ROWS), 2 * ROWS)
        term = lax.dot_general(
            fin[0, :, columns], fin[1], (((0,), (0,)), ((), ())), preferred_element_type=F32
        )
        part[t] = (term * factor).astype(BF16)
        to_core(t).start()

    @pl.when(d == 0)
    def _():
        build()

    def pair(t, rows=slice(0, ROWS)):
        own = part[t, mine, :][rows]
        return own.astype(F32) + corein[t, rows, :].astype(F32)

    def ring(src, dst, s, target):
        return pltpu.make_async_remote_copy(
            src_ref=src,
            dst_ref=dst,
            send_sem=x_send.at[s],
            recv_sem=x_recv.at[s],
            device_id={"freq": target},
            device_id_type=MESH,
        )

    low, high = slice(0, ROWS // 2), slice(ROWS // 2, ROWS)
    copies = {}
    for q in (0, 1):
        base = 6 * q
        lo, hi = pl.ds(0, ROWS // 2), pl.ds(ROWS // 2, ROWS // 2)
        copies[q] = dict(
            two_up=ring(two.at[q, lo, :], rel_up.at[q], base, up),
            two_down=ring(two.at[q, hi, :], rel_down.at[q], base + 1, down),
            one_now=ring(one.at[q, hi, :], from_down.at[q, hi, :], base + 2, up),
            one_late=ring(one.at[q, lo, :], from_down.at[q, lo, :], base + 3, up),
            three_now=ring(three.at[q, lo, :], from_up.at[q, lo, :], base + 4, down),
            three_late=ring(three.at[q, hi, :], from_up.at[q, hi, :], base + 5, down),
        )

    def far(q):
        t = ORDER.index((q, 2))
        to_core(t).wait_recv()
        two[q] = pair(t).astype(BF16)
        copies[q]["two_up"].start()
        copies[q]["two_down"].start()

    def near(q):
        t = ORDER.index((q, 1))
        to_core(t).wait_recv()
        one[q] = pair(t).astype(BF16)
        copies[q]["one_now"].start()
        t = ORDER.index((q, 3))
        to_core(t).wait_recv()
        three[q] = pair(t).astype(BF16)
        copies[q]["three_now"].start()

    def relay(q):
        copies[q]["two_up"].wait_recv()
        one[q, low, :] = (one[q, low, :].astype(F32) + rel_up[q].astype(F32)).astype(BF16)
        copies[q]["one_late"].start()
        copies[q]["two_down"].wait_recv()
        three[q, high, :] = (three[q, high, :].astype(F32) + rel_down[q].astype(F32)).astype(BF16)
        copies[q]["three_late"].start()

    def collect(q):
        t = ORDER.index((q, 0))
        to_core(t).wait_recv()
        for name in ("one_now", "three_now", "one_late", "three_late"):
            copies[q][name].wait_recv()
        return pair(t) + from_down[q].astype(F32) + from_up[q].astype(F32)

    over = pltpu.make_async_remote_copy(
        src_ref=ysend, dst_ref=yin, send_sem=y_send, recv_sem=y_recv,
        device_id={"freq": across}, device_id_type=MESH,
    )
    far(1)
    near(1)
    far(0)
    relay(1)
    near(0)
    ysend[...] = collect(1).astype(BF16)
    over.start()
    relay(0)
    acc[...] = collect(0)
    over.wait_recv()
    acc[...] = acc[...] + yin[...].astype(F32)
    for k in range(DEPTHS):
        pieces[k] = acc[PIECE * k : PIECE * (k + 1), :].astype(BF16)

    def deal(k):
        target = (d + k) % DEPTHS
        return pltpu.make_async_remote_copy(
            src_ref=pieces.at[target],
            dst_ref=gath.at[d],
            send_sem=d_send.at[k],
            recv_sem=d_recv.at[k],
            device_id={"depth": target},
            device_id_type=MESH,
        )

    def arrival(k):
        source = (d + DEPTHS - k) % DEPTHS
        return pltpu.make_async_remote_copy(
            src_ref=pieces.at[source],
            dst_ref=gath.at[source],
            send_sem=d_send.at[k],
            recv_sem=d_recv.at[k],
            device_id={"depth": source},
            device_id_type=MESH,
        )

    def send_piece(k, carry):
        deal(k).start()
        return carry

    lax.fori_loop(1, DEPTHS, send_piece, 0)
    gath[d] = pieces[d]

    def take_piece(k, carry):
        arrival(k).wait_recv()
        return carry

    lax.fori_loop(1, DEPTHS, take_piece, 0)
    for k in range(DEPTHS):
        xs[PIECE * k : PIECE * (k + 1), :] = gath[k].astype(F32)

    def stack(lag, carry):
        term = jnp.dot(xs[...].astype(BF16), sel[lag], preferred_element_type=F32)
        g[lag, 0, 0:ROWS, :] = term[:, :LANES]
        g[lag, 1, 0:ROWS, :] = term[:, LANES:]
        return carry

    lax.fori_loop(0, DEPTHS, stack, 0)
    scale = 1.0 / math.sqrt(POINTS)
    for row in range(PIECE):
        for side in range(2):
            total = g[0, side, pl.ds(row, DEPTHS, stride=PIECE), :]
            for lag in range(1, DEPTHS):
                total = total + g[lag, side, pl.ds(PIECE * lag + row, DEPTHS, stride=PIECE), :]
            out_ref[row, :, LANES * side : LANES * (side + 1)] = total * scale

    @pl.when(d < DEPTHS - 1)
    def _():
        def drain(b, carry):
            hop(b).wait_send()
            return carry

        lax.fori_loop(0, BATCHES, drain, 0)

    for t in range(len(ORDER)):
        to_core(t).wait_send()
    for q in (0, 1):
        for copy in copies[q].values():
            copy.wait_send()
    over.wait_send()

    def drain_piece(k, carry):
        deal(k).wait_send()
        return carry

    lax.fori_loop(1, DEPTHS, drain_piece, 0)


def migrate(extrap, packed, factor, angle_lag):
    vmem = pl.BlockSpec(memory_space=pltpu.VMEM)
    return pl.pallas_call(
        kernel,
        out_shape=jax.ShapeDtypeStruct((PIECE, DEPTHS, ANGLES), F32),
        in_specs=[
            pl.BlockSpec(memory_space=pl.ANY),
            vmem,
            pl.BlockSpec(memory_space=pltpu.SMEM),
            vmem,
        ],
        out_specs=vmem,
        scratch_shapes=[
            pltpu.VMEM((2, POINTS, POINTS), BF16),
            pltpu.VMEM((2, 2 * SHOTS, POINTS), BF16),
            pltpu.VMEM((2, 2 * SHOTS, POINTS), BF16),
            pltpu.VMEM((DEPTHS, POINTS, ANGLES), BF16),
            pltpu.VMEM((8, 2 * ROWS, POINTS), BF16),
            pltpu.VMEM((8, ROWS, POINTS), BF16),
            pltpu.VMEM((2, ROWS, POINTS), BF16),
            pltpu.VMEM((2, ROWS, POINTS), BF16),
            pltpu.VMEM((2, ROWS, POINTS), BF16),
            pltpu.VMEM((2, ROWS // 2, POINTS), BF16),
            pltpu.VMEM((2, ROWS // 2, POINTS), BF16),
            pltpu.VMEM((2, ROWS, POINTS), BF16),
            pltpu.VMEM((2, ROWS, POINTS), BF16),
            pltpu.VMEM((ROWS, POINTS), BF16),
            pltpu.VMEM((ROWS, POINTS), BF16),
            pltpu.VMEM((ROWS, POINTS), F32),
            pltpu.VMEM((DEPTHS, PIECE, POINTS), BF16),
            pltpu.VMEM((DEPTHS, PIECE, POINTS), BF16),
            pltpu.VMEM((ROWS, POINTS), F32),
            pltpu.VMEM((DEPTHS, 2, 2 * ROWS, LANES), F32),
            pltpu.SemaphoreType.DMA,
            pltpu.SemaphoreType.DMA((BATCHES,)),
            pltpu.SemaphoreType.DMA((BATCHES,)),
            pltpu.SemaphoreType.DMA((8,)),
            pltpu.SemaphoreType.DMA((8,)),
            pltpu.SemaphoreType.DMA((12,)),
            pltpu.SemaphoreType.DMA((12,)),
            pltpu.SemaphoreType.DMA,
            pltpu.SemaphoreType.DMA,
            pltpu.SemaphoreType.DMA((DEPTHS,)),
            pltpu.SemaphoreType.DMA((DEPTHS,)),
        ],
        compiler_params=pltpu.CompilerParams(
            collective_id=0, has_side_effects=True, vmem_limit_bytes=48 * 1024 * 1024
        ),
        name="migrate",
    )(extrap, packed, factor, angle_lag)


def shards(extrap, source_field, record_field, shot_of_record, freq_index, angle_lag):
    freq_count = lax.axis_size("freq")
    paired = source_field[0].at[shot_of_record].get(mode="promise_in_bounds")

    def pack(field):
        split = field.reshape(BATCHES, BATCH, 2, POINTS)
        return split.transpose(0, 2, 1, 3).reshape(2 * SHOTS, POINTS)

    packed = jnp.stack([pack(paired), pack(record_field[0])])
    factor = (
        (freq_index.astype(F32) + 1.0) / (8 * freq_count) / math.sqrt(SHOTS * freq_count)
    )
    return migrate(extrap[0, 0], packed, factor, angle_lag)


def solution(mesh):
    placed = (
        P("depth", "freq", None, None, None),
        P("freq", None, None, None),
        P("freq", None, None, None),
        P(),
        P("freq"),
        P(),
    )
    return jax.shard_map(
        shards,
        mesh=mesh,
        in_specs=placed,
        out_specs=P(("freq", "depth"), None, None),
        check_vma=False,
    )
```

```python
import math

import jax
import jax.numpy as jnp
from jax import lax
from jax.experimental import pallas as pl
from jax.experimental.pallas import tpu as pltpu
from jax.sharding import PartitionSpec as P

MESH = pl.DeviceIdType.MESH
BATCH = 4
DEPTHS = 16
ROWS = 64
POINTS = 1024
ANGLES = 256
SHOTS = 128
LANES = 128
BATCHES = SHOTS // BATCH
HALF = 2 * BATCH
PIECE = ROWS // DEPTHS
ORDER = [(1, 2), (1, 1), (1, 3), (1, 0), (0, 2), (0, 1), (0, 3), (0, 0)]
F32 = jnp.float32
BF16 = jnp.bfloat16


def swap_parts(a, b):
    rolled = jnp.concatenate(
        [pltpu.roll(b[:HALF], BATCH, 0), pltpu.roll(b[HALF:], BATCH, 0)], axis=0
    )
    row = lax.broadcasted_iota(jnp.int32, rolled.shape, 0)
    minus = (row < BATCH) | (row >= HALF + BATCH)
    return a + jnp.where(minus, -rolled, rolled)


def expand(part):
    shape = (SHOTS, 2 * SHOTS)
    shot = lax.broadcasted_iota(jnp.int32, shape, 0)
    row = lax.broadcasted_iota(jnp.int32, shape, 1)
    place = row - BATCH * part
    hit = (place >= 0) & (place % HALF < BATCH) & ((place // HALF) * BATCH + place % HALF == shot)
    return jnp.where(hit, 1.0, 0.0).astype(BF16)


def kernel(
    e_hbm, x_ref, shot_ref, factor_ref, lag_ref, out_ref,
    e_ref, inbuf, fin, field, sel, part, corein, two, one, three, rel_up, rel_down, from_down, from_up,
    ysend, yin, acc, pieces, gath, xs, g,
    e_sem, chain_send, chain_recv, core_send, core_recv, x_send, x_recv, y_send, y_recv, d_send, d_recv, greet_sem,
):
    d = lax.axis_index("depth")
    f = lax.axis_index("freq")
    core = f % 2
    x = (f // 2) % 4
    yh = f // 8
    partner = f + 1 - 2 * core
    up = yh * 8 + ((x + 1) % 4) * 2 + core
    down = yh * 8 + ((x + 3) % 4) * 2 + core
    across = f + 8 - 16 * yh

    load_e = pltpu.make_async_copy(e_hbm, e_ref, e_sem)
    load_e.start()
    barrier = pltpu.get_barrier_semaphore()
    for other in (partner, up, down, across):
        pl.semaphore_signal(barrier, inc=1, device_id={"freq": other}, device_id_type=MESH)

    @pl.when(d > 0)
    def _():
        pl.semaphore_signal(barrier, inc=1, device_id={"depth": d - 1}, device_id_type=MESH)

    def build():
        def one_lag(lag, carry):
            sel[lag] = jnp.where(lag_ref[...] == lag, 1.0, 0.0).astype(BF16)
            g[lag, :, ROWS:, :] = jnp.zeros((2, ROWS, LANES), F32)
            return carry

        lax.fori_loop(0, DEPTHS, one_lag, 0)

    @pl.when(d > 0)
    def _():
        build()

    @pl.when(d == 0)
    def _():
        shot = lax.broadcasted_iota(jnp.int32, (SHOTS, SHOTS), 0)
        chosen = jnp.where(shot == shot_ref[...], 1.0, 0.0).astype(BF16)
        ways = [expand(0), expand(1)]
        contract = (((0,), (0,)), ((), ()))
        packed = []
        for kind in range(2):
            total = None
            for half in range(2):
                way = ways[half]
                if kind == 0:
                    way = jnp.dot(chosen, way, preferred_element_type=F32).astype(BF16)
                term = lax.dot_general(
                    way, x_ref[kind, half], contract, preferred_element_type=F32
                )
                total = term if total is None else total + term
            packed.append(total.reshape(BATCHES, HALF, POINTS))
        inbuf[...] = jnp.concatenate(packed, axis=1).astype(BF16)

    load_e.wait()

    @pl.when(d < DEPTHS - 1)
    def _():
        pl.semaphore_wait(barrier, 5)

    @pl.when(d == DEPTHS - 1)
    def _():
        pl.semaphore_wait(barrier, 4)

    def hop(b):
        return pltpu.make_async_remote_copy(
            src_ref=fin.at[b],
            dst_ref=inbuf.at[b],
            send_sem=chain_send.at[b],
            recv_sem=chain_recv.at[b],
            device_id={"depth": d + 1},
            device_id_type=MESH,
        )

    def step(b):
        @pl.when(d > 0)
        def _():
            hop(b).wait_recv()

        values = inbuf[b]
        first = jnp.dot(values, e_ref[0], preferred_element_type=F32)
        second = jnp.dot(values, e_ref[1], preferred_element_type=F32)
        result = swap_parts(first, second)
        fin[b] = result.astype(BF16)

        @pl.when(d < DEPTHS - 1)
        def _():
            hop(b).start()

        return result

    def two_steps(p, carry):
        even = step(2 * p)
        odd = step(2 * p + 1)
        rows = pl.ds(pl.multiple_of(p * 2 * HALF, 2 * HALF), 2 * HALF)
        field[0, rows, :] = jnp.concatenate([even[:HALF], odd[:HALF]], axis=0).astype(BF16)
        field[1, rows, :] = jnp.concatenate([even[HALF:], odd[HALF:]], axis=0).astype(BF16)
        return carry

    two_steps(0, 0)

    def greet(k, carry):
        pl.semaphore_signal(greet_sem, inc=1, device_id={"depth": k}, device_id_type=MESH)
        return carry

    lax.fori_loop(0, d, greet, 0)
    lax.fori_loop(1, BATCHES // 2, two_steps, 0)

    mine = pl.ds(pl.multiple_of(core * ROWS, ROWS), ROWS)
    theirs = pl.ds(pl.multiple_of((1 - core) * ROWS, ROWS), ROWS)

    def to_core(t):
        return pltpu.make_async_remote_copy(
            src_ref=part.at[t, theirs, :],
            dst_ref=corein.at[t],
            send_sem=core_send.at[t],
            recv_sem=core_recv.at[t],
            device_id={"freq": partner},
            device_id_type=MESH,
        )

    factor = factor_ref[0]
    for t, (q, r) in enumerate(ORDER):
        block = (yh + q * (1 - 2 * yh)) * 4 + (x + r) % 4
        columns = pl.ds(pl.multiple_of(block * 2 * ROWS, 2 * ROWS), 2 * ROWS)
        term = lax.dot_general(
            field[0, :, columns], field[1], (((0,), (0,)), ((), ())), preferred_element_type=F32
        )
        part[t] = (term * factor).astype(BF16)
        to_core(t).start()

    @pl.when(d == 0)
    def _():
        build()

    def pair(t, rows=slice(0, ROWS)):
        own = part[t, mine, :][rows]
        return own.astype(F32) + corein[t, rows, :].astype(F32)

    def ring(src, dst, s, target):
        return pltpu.make_async_remote_copy(
            src_ref=src,
            dst_ref=dst,
            send_sem=x_send.at[s],
            recv_sem=x_recv.at[s],
            device_id={"freq": target},
            device_id_type=MESH,
        )

    low, high = slice(0, ROWS // 2), slice(ROWS // 2, ROWS)
    copies = {}
    for q in (0, 1):
        base = 6 * q
        lo, hi = pl.ds(0, ROWS // 2), pl.ds(ROWS // 2, ROWS // 2)
        copies[q] = dict(
            two_up=ring(two.at[q, lo, :], rel_up.at[q], base, up),
            two_down=ring(two.at[q, hi, :], rel_down.at[q], base + 1, down),
            one_now=ring(one.at[q, hi, :], from_down.at[q, hi, :], base + 2, up),
            one_late=ring(one.at[q, lo, :], from_down.at[q, lo, :], base + 3, up),
            three_now=ring(three.at[q, lo, :], from_up.at[q, lo, :], base + 4, down),
            three_late=ring(three.at[q, hi, :], from_up.at[q, hi, :], base + 5, down),
        )

    def far(q):
        t = ORDER.index((q, 2))
        to_core(t).wait_recv()
        two[q] = pair(t).astype(BF16)
        copies[q]["two_up"].start()
        copies[q]["two_down"].start()

    def near(q):
        t = ORDER.index((q, 1))
        to_core(t).wait_recv()
        one[q] = pair(t).astype(BF16)
        copies[q]["one_now"].start()
        t = ORDER.index((q, 3))
        to_core(t).wait_recv()
        three[q] = pair(t).astype(BF16)
        copies[q]["three_now"].start()

    def relay(q):
        copies[q]["two_up"].wait_recv()
        one[q, low, :] = (one[q, low, :].astype(F32) + rel_up[q].astype(F32)).astype(BF16)
        copies[q]["one_late"].start()
        copies[q]["two_down"].wait_recv()
        three[q, high, :] = (three[q, high, :].astype(F32) + rel_down[q].astype(F32)).astype(BF16)
        copies[q]["three_late"].start()

    def collect(q):
        t = ORDER.index((q, 0))
        to_core(t).wait_recv()
        for name in ("one_now", "three_now", "one_late", "three_late"):
            copies[q][name].wait_recv()
        return pair(t) + from_down[q].astype(F32) + from_up[q].astype(F32)

    over = pltpu.make_async_remote_copy(
        src_ref=ysend, dst_ref=yin, send_sem=y_send, recv_sem=y_recv,
        device_id={"freq": across}, device_id_type=MESH,
    )
    far(1)
    near(1)
    far(0)
    relay(1)
    near(0)
    ysend[...] = collect(1).astype(BF16)
    over.start()
    relay(0)
    acc[...] = collect(0)
    over.wait_recv()
    acc[...] = acc[...] + yin[...].astype(F32)
    for k in range(DEPTHS):
        pieces[k] = acc[PIECE * k : PIECE * (k + 1), :].astype(BF16)

    def deal(k):
        target = (d + k) % DEPTHS
        return pltpu.make_async_remote_copy(
            src_ref=pieces.at[target],
            dst_ref=gath.at[d],
            send_sem=d_send.at[k],
            recv_sem=d_recv.at[k],
            device_id={"depth": target},
            device_id_type=MESH,
        )

    def arrival(k):
        source = (d + DEPTHS - k) % DEPTHS
        return pltpu.make_async_remote_copy(
            src_ref=pieces.at[source],
            dst_ref=gath.at[source],
            send_sem=d_send.at[k],
            recv_sem=d_recv.at[k],
            device_id={"depth": source},
            device_id_type=MESH,
        )

    def send_piece(k, carry):
        deal(k).start()
        return carry


    @pl.when(d < DEPTHS - 1)
    def _():
        pl.semaphore_wait(greet_sem, DEPTHS - 1 - d)

    lax.fori_loop(1, DEPTHS, send_piece, 0)
    gath[d] = pieces[d]

    def take_piece(k, carry):
        arrival(k).wait_recv()
        return carry

    lax.fori_loop(1, DEPTHS, take_piece, 0)
    for k in range(DEPTHS):
        xs[PIECE * k : PIECE * (k + 1), :] = gath[k].astype(F32)

    def stack(lag, carry):
        term = jnp.dot(xs[...].astype(BF16), sel[lag], preferred_element_type=F32)
        g[lag, 0, 0:ROWS, :] = term[:, :LANES]
        g[lag, 1, 0:ROWS, :] = term[:, LANES:]
        return carry

    lax.fori_loop(0, DEPTHS, stack, 0)
    scale = 1.0 / math.sqrt(POINTS)
    for row in range(PIECE):
        for side in range(2):
            total = g[0, side, pl.ds(row, DEPTHS, stride=PIECE), :]
            for lag in range(1, DEPTHS):
                total = total + g[lag, side, pl.ds(PIECE * lag + row, DEPTHS, stride=PIECE), :]
            out_ref[row, :, LANES * side : LANES * (side + 1)] = total * scale

    @pl.when(d < DEPTHS - 1)
    def _():
        def drain(b, carry):
            hop(b).wait_send()
            return carry

        lax.fori_loop(0, BATCHES, drain, 0)

    for t in range(len(ORDER)):
        to_core(t).wait_send()
    for q in (0, 1):
        for copy in copies[q].values():
            copy.wait_send()
    over.wait_send()

    def drain_piece(k, carry):
        deal(k).wait_send()
        return carry

    lax.fori_loop(1, DEPTHS, drain_piece, 0)


def migrate(extrap, fields, shots, factor, angle_lag):
    vmem = pl.BlockSpec(memory_space=pltpu.VMEM)
    return pl.pallas_call(
        kernel,
        out_shape=jax.ShapeDtypeStruct((PIECE, DEPTHS, ANGLES), F32),
        in_specs=[
            pl.BlockSpec(memory_space=pl.ANY),
            vmem,
            vmem,
            pl.BlockSpec(memory_space=pltpu.SMEM),
            vmem,
        ],
        out_specs=vmem,
        scratch_shapes=[
            pltpu.VMEM((2, POINTS, POINTS), BF16),
            pltpu.VMEM((BATCHES, 2 * HALF, POINTS), BF16),
            pltpu.VMEM((BATCHES, 2 * HALF, POINTS), BF16),
            pltpu.VMEM((2, 2 * SHOTS, POINTS), BF16),
            pltpu.VMEM((DEPTHS, POINTS, ANGLES), BF16),
            pltpu.VMEM((8, 2 * ROWS, POINTS), BF16),
            pltpu.VMEM((8, ROWS, POINTS), BF16),
            pltpu.VMEM((2, ROWS, POINTS), BF16),
            pltpu.VMEM((2, ROWS, POINTS), BF16),
            pltpu.VMEM((2, ROWS, POINTS), BF16),
            pltpu.VMEM((2, ROWS // 2, POINTS), BF16),
            pltpu.VMEM((2, ROWS // 2, POINTS), BF16),
            pltpu.VMEM((2, ROWS, POINTS), BF16),
            pltpu.VMEM((2, ROWS, POINTS), BF16),
            pltpu.VMEM((ROWS, POINTS), BF16),
            pltpu.VMEM((ROWS, POINTS), BF16),
            pltpu.VMEM((ROWS, POINTS), F32),
            pltpu.VMEM((DEPTHS, PIECE, POINTS), BF16),
            pltpu.VMEM((DEPTHS, PIECE, POINTS), BF16),
            pltpu.VMEM((ROWS, POINTS), F32),
            pltpu.VMEM((DEPTHS, 2, 2 * ROWS, LANES), F32),
            pltpu.SemaphoreType.DMA,
            pltpu.SemaphoreType.DMA((BATCHES,)),
            pltpu.SemaphoreType.DMA((BATCHES,)),
            pltpu.SemaphoreType.DMA((8,)),
            pltpu.SemaphoreType.DMA((8,)),
            pltpu.SemaphoreType.DMA((12,)),
            pltpu.SemaphoreType.DMA((12,)),
            pltpu.SemaphoreType.DMA,
            pltpu.SemaphoreType.DMA,
            pltpu.SemaphoreType.DMA((DEPTHS,)),
            pltpu.SemaphoreType.DMA((DEPTHS,)),
            pltpu.SemaphoreType.REGULAR,
        ],
        compiler_params=pltpu.CompilerParams(
            collective_id=0, has_side_effects=True, vmem_limit_bytes=48 * 1024 * 1024
        ),
        name="migrate",
    )(extrap, fields, shots, factor, angle_lag)


def shards(extrap, source_field, record_field, shot_of_record, freq_index, angle_lag):
    freq_count = lax.axis_size("freq")
    fields = jnp.stack([source_field[0], record_field[0]]).transpose(0, 2, 1, 3)
    factor = (
        (freq_index.astype(F32) + 1.0) / (8 * freq_count) / math.sqrt(SHOTS * freq_count)
    )
    return migrate(extrap[0, 0], fields, shot_of_record.reshape(1, SHOTS), factor, angle_lag)


def solution(mesh):
    placed = (
        P("depth", "freq", None, None, None),
        P("freq", None, None, None),
        P("freq", None, None, None),
        P(),
        P("freq"),
        P(),
    )
    return jax.shard_map(
        shards,
        mesh=mesh,
        in_specs=placed,
        out_specs=P(("freq", "depth"), None, None),
        check_vma=False,
    )
```

```python
import math

import jax
import jax.numpy as jnp
from jax import lax
from jax.experimental import pallas as pl
from jax.experimental.pallas import tpu as pltpu
from jax.sharding import PartitionSpec as P

MESH = pl.DeviceIdType.MESH
BATCH = 4
DEPTHS = 16
ROWS = 64
POINTS = 1024
ANGLES = 256
SHOTS = 128
LANES = 128
BATCHES = SHOTS // BATCH
HALF = 2 * BATCH
PIECE = ROWS // DEPTHS
ORDER = [(1, 2), (1, 1), (1, 3), (1, 0), (0, 2), (0, 1), (0, 3), (0, 0)]
F32 = jnp.float32
BF16 = jnp.bfloat16


def swap_parts(a, b):
    rolled = jnp.concatenate(
        [pltpu.roll(b[:HALF], BATCH, 0), pltpu.roll(b[HALF:], BATCH, 0)], axis=0
    )
    row = lax.broadcasted_iota(jnp.int32, rolled.shape, 0)
    minus = (row < BATCH) | (row >= HALF + BATCH)
    return a + jnp.where(minus, -rolled, rolled)


def expand(part):
    shape = (SHOTS, 2 * SHOTS)
    shot = lax.broadcasted_iota(jnp.int32, shape, 0)
    row = lax.broadcasted_iota(jnp.int32, shape, 1)
    hit = ((row // HALF) * BATCH + row % BATCH == shot) & ((row % HALF) // BATCH == part)
    return jnp.where(hit, 1.0, 0.0).astype(BF16)


def spread(shots, part):
    line = lax.broadcasted_iota(jnp.int32, (2 * SHOTS, SHOTS), 0)
    return jnp.where(2 * shots + part == line, 1.0, 0.0).astype(BF16)


def route(shots):
    total = jnp.dot(spread(shots, 0), expand(0), preferred_element_type=F32)
    total = total + jnp.dot(spread(shots, 1), expand(1), preferred_element_type=F32)
    return total.astype(BF16)


def kernel(
    e_hbm, source_hbm, record_hbm, shot_hbm, factor_ref, lag_hbm, out_ref,
    e_ref, source_ref, record_ref, shot_ref, lag_ref, inbuf, fin, field, sel, part, corein, two, one, three, rel_up, rel_down, from_down, from_up,
    ysend, yin, acc, pieces, gath, xs, g,
    e_sem, lag_sem, raw_sem, chain_send, chain_recv, core_send, core_recv, x_send, x_recv, y_send, y_recv, d_send, d_recv, greet_sem,
):
    d = lax.axis_index("depth")
    f = lax.axis_index("freq")
    core = f % 2
    x = (f // 2) % 4
    yh = f // 8
    partner = f + 1 - 2 * core
    up = yh * 8 + ((x + 1) % 4) * 2 + core
    down = yh * 8 + ((x + 3) % 4) * 2 + core
    across = f + 8 - 16 * yh

    load_e = pltpu.make_async_copy(e_hbm, e_ref, e_sem)
    load_e.start()
    load_lag = pltpu.make_async_copy(lag_hbm, lag_ref, lag_sem)
    load_lag.start()
    raw = [
        pltpu.make_async_copy(shot_hbm, shot_ref, raw_sem.at[0]),
        pltpu.make_async_copy(source_hbm, source_ref, raw_sem.at[1]),
        pltpu.make_async_copy(record_hbm, record_ref, raw_sem.at[2]),
    ]

    @pl.when(d == 0)
    def _():
        for load in raw:
            load.start()

    barrier = pltpu.get_barrier_semaphore()
    for other in (partner, up, down, across):
        pl.semaphore_signal(barrier, inc=1, device_id={"freq": other}, device_id_type=MESH)

    @pl.when(d > 0)
    def _():
        pl.semaphore_signal(barrier, inc=1, device_id={"depth": d - 1}, device_id_type=MESH)

    def build():
        load_lag.wait()

        def one_lag(lag, carry):
            sel[lag] = jnp.where(lag_ref[...] == lag, 1.0, 0.0).astype(BF16)
            g[lag, :, ROWS:, :] = jnp.zeros((2, ROWS, LANES), F32)
            return carry

        lax.fori_loop(0, DEPTHS, one_lag, 0)

    @pl.when(d > 0)
    def _():
        build()

    @pl.when(d == 0)
    def _():
        for load in raw:
            load.wait()
        straight = lax.broadcasted_iota(jnp.int32, (1, SHOTS), 1)
        packed = []
        for field_ref, shots in ((source_ref, shot_ref[...]), (record_ref, straight)):
            lines = field_ref[...].reshape(2 * SHOTS, POINTS)
            rows = lax.dot_general(
                route(shots), lines, (((0,), (0,)), ((), ())), preferred_element_type=F32
            )
            packed.append(rows.reshape(BATCHES, HALF, POINTS))
        inbuf[...] = jnp.concatenate(packed, axis=1).astype(BF16)

    load_e.wait()

    @pl.when(d < DEPTHS - 1)
    def _():
        pl.semaphore_wait(barrier, 5)

    @pl.when(d == DEPTHS - 1)
    def _():
        pl.semaphore_wait(barrier, 4)

    side = POINTS // 2
    sides = [slice(0, side), slice(side, POINTS)]

    def hop(b, n):
        columns = pl.ds(n * side, side)
        return pltpu.make_async_remote_copy(
            src_ref=fin.at[b, :, columns],
            dst_ref=inbuf.at[b, :, columns],
            send_sem=chain_send.at[2 * b + n],
            recv_sem=chain_recv.at[2 * b + n],
            device_id={"depth": d + 1},
            device_id_type=MESH,
        )

    def step(b):
        @pl.when(d > 0)
        def _():
            hop(b, 0).wait_recv()

        values = inbuf[b, :, sides[0]]
        first = jnp.dot(values, e_ref[0, sides[0], :], preferred_element_type=F32)
        second = jnp.dot(values, e_ref[1, sides[0], :], preferred_element_type=F32)

        @pl.when(d > 0)
        def _():
            hop(b, 1).wait_recv()

        values = inbuf[b, :, sides[1]]
        results = []
        for n in range(2):
            part_first = first[:, sides[n]] + jnp.dot(
                values, e_ref[0, sides[1], sides[n]], preferred_element_type=F32
            )
            part_second = second[:, sides[n]] + jnp.dot(
                values, e_ref[1, sides[1], sides[n]], preferred_element_type=F32
            )
            result = swap_parts(part_first, part_second)
            fin[b, :, sides[n]] = result.astype(BF16)

            @pl.when(d < DEPTHS - 1)
            def _():
                hop(b, n).start()

            results.append(result)
        return results

    def two_steps(p, carry):
        even = step(2 * p)
        odd = step(2 * p + 1)
        rows = pl.ds(pl.multiple_of(p * 2 * HALF, 2 * HALF), 2 * HALF)
        for n in range(2):
            field[0, rows, sides[n]] = jnp.concatenate(
                [even[n][:HALF], odd[n][:HALF]], axis=0
            ).astype(BF16)
            field[1, rows, sides[n]] = jnp.concatenate(
                [even[n][HALF:], odd[n][HALF:]], axis=0
            ).astype(BF16)
        return carry

    two_steps(0, 0)

    def greet(k, carry):
        pl.semaphore_signal(greet_sem, inc=1, device_id={"depth": k}, device_id_type=MESH)
        return carry

    lax.fori_loop(0, d, greet, 0)
    lax.fori_loop(1, BATCHES // 2, two_steps, 0)

    mine = pl.ds(pl.multiple_of(core * ROWS, ROWS), ROWS)
    theirs = pl.ds(pl.multiple_of((1 - core) * ROWS, ROWS), ROWS)

    def to_core(t):
        return pltpu.make_async_remote_copy(
            src_ref=part.at[t, theirs, :],
            dst_ref=corein.at[t],
            send_sem=core_send.at[t],
            recv_sem=core_recv.at[t],
            device_id={"freq": partner},
            device_id_type=MESH,
        )

    factor = factor_ref[0]
    for t, (q, r) in enumerate(ORDER):
        block = (yh + q * (1 - 2 * yh)) * 4 + (x + r) % 4
        columns = pl.ds(pl.multiple_of(block * 2 * ROWS, 2 * ROWS), 2 * ROWS)
        term = lax.dot_general(
            field[0, :, columns], field[1], (((0,), (0,)), ((), ())), preferred_element_type=F32
        )
        part[t] = (term * factor).astype(BF16)
        to_core(t).start()

    @pl.when(d == 0)
    def _():
        build()

    def pair(t, rows=slice(0, ROWS)):
        own = part[t, mine, :][rows]
        return own.astype(F32) + corein[t, rows, :].astype(F32)

    def ring(src, dst, s, target):
        return pltpu.make_async_remote_copy(
            src_ref=src,
            dst_ref=dst,
            send_sem=x_send.at[s],
            recv_sem=x_recv.at[s],
            device_id={"freq": target},
            device_id_type=MESH,
        )

    low, high = slice(0, ROWS // 2), slice(ROWS // 2, ROWS)
    copies = {}
    for q in (0, 1):
        base = 6 * q
        lo, hi = pl.ds(0, ROWS // 2), pl.ds(ROWS // 2, ROWS // 2)
        copies[q] = dict(
            two_up=ring(two.at[q, lo, :], rel_up.at[q], base, up),
            two_down=ring(two.at[q, hi, :], rel_down.at[q], base + 1, down),
            one_now=ring(one.at[q, hi, :], from_down.at[q, hi, :], base + 2, up),
            one_late=ring(one.at[q, lo, :], from_down.at[q, lo, :], base + 3, up),
            three_now=ring(three.at[q, lo, :], from_up.at[q, lo, :], base + 4, down),
            three_late=ring(three.at[q, hi, :], from_up.at[q, hi, :], base + 5, down),
        )

    def far(q):
        t = ORDER.index((q, 2))
        to_core(t).wait_recv()
        two[q] = pair(t).astype(BF16)
        copies[q]["two_up"].start()
        copies[q]["two_down"].start()

    def near(q):
        t = ORDER.index((q, 1))
        to_core(t).wait_recv()
        one[q] = pair(t).astype(BF16)
        copies[q]["one_now"].start()
        t = ORDER.index((q, 3))
        to_core(t).wait_recv()
        three[q] = pair(t).astype(BF16)
        copies[q]["three_now"].start()

    def relay(q):
        copies[q]["two_up"].wait_recv()
        one[q, low, :] = (one[q, low, :].astype(F32) + rel_up[q].astype(F32)).astype(BF16)
        copies[q]["one_late"].start()
        copies[q]["two_down"].wait_recv()
        three[q, high, :] = (three[q, high, :].astype(F32) + rel_down[q].astype(F32)).astype(BF16)
        copies[q]["three_late"].start()

    def collect(q):
        t = ORDER.index((q, 0))
        to_core(t).wait_recv()
        for name in ("one_now", "three_now", "one_late", "three_late"):
            copies[q][name].wait_recv()
        return pair(t) + from_down[q].astype(F32) + from_up[q].astype(F32)

    over = pltpu.make_async_remote_copy(
        src_ref=ysend, dst_ref=yin, send_sem=y_send, recv_sem=y_recv,
        device_id={"freq": across}, device_id_type=MESH,
    )
    far(1)
    near(1)
    far(0)
    relay(1)
    near(0)
    ysend[...] = collect(1).astype(BF16)
    over.start()
    relay(0)
    acc[...] = collect(0)
    over.wait_recv()
    acc[...] = acc[...] + yin[...].astype(F32)
    for k in range(DEPTHS):
        pieces[k] = acc[PIECE * k : PIECE * (k + 1), :].astype(BF16)

    def deal(k):
        target = (d + k) % DEPTHS
        return pltpu.make_async_remote_copy(
            src_ref=pieces.at[target],
            dst_ref=gath.at[d],
            send_sem=d_send.at[k],
            recv_sem=d_recv.at[k],
            device_id={"depth": target},
            device_id_type=MESH,
        )

    def arrival(k):
        source = (d + DEPTHS - k) % DEPTHS
        return pltpu.make_async_remote_copy(
            src_ref=pieces.at[source],
            dst_ref=gath.at[source],
            send_sem=d_send.at[k],
            recv_sem=d_recv.at[k],
            device_id={"depth": source},
            device_id_type=MESH,
        )

    def send_piece(k, carry):
        deal(k).start()
        return carry


    @pl.when(d < DEPTHS - 1)
    def _():
        pl.semaphore_wait(greet_sem, DEPTHS - 1 - d)

    lax.fori_loop(1, DEPTHS, send_piece, 0)
    gath[d] = pieces[d]

    def take_piece(k, carry):
        arrival(k).wait_recv()
        return carry

    lax.fori_loop(1, DEPTHS, take_piece, 0)
    for k in range(DEPTHS):
        xs[PIECE * k : PIECE * (k + 1), :] = gath[k].astype(F32)

    def stack(lag, carry):
        term = jnp.dot(xs[...].astype(BF16), sel[lag], preferred_element_type=F32)
        g[lag, 0, 0:ROWS, :] = term[:, :LANES]
        g[lag, 1, 0:ROWS, :] = term[:, LANES:]
        return carry

    lax.fori_loop(0, DEPTHS, stack, 0)
    scale = 1.0 / math.sqrt(POINTS)
    for row in range(PIECE):
        for wing in range(2):
            total = g[0, wing, pl.ds(row, DEPTHS, stride=PIECE), :]
            for lag in range(1, DEPTHS):
                total = total + g[lag, wing, pl.ds(PIECE * lag + row, DEPTHS, stride=PIECE), :]
            out_ref[row, :, LANES * wing : LANES * (wing + 1)] = total * scale

    @pl.when(d < DEPTHS - 1)
    def _():
        def drain(b, carry):
            hop(b, 0).wait_send()
            hop(b, 1).wait_send()
            return carry

        lax.fori_loop(0, BATCHES, drain, 0)

    for t in range(len(ORDER)):
        to_core(t).wait_send()
    for q in (0, 1):
        for copy in copies[q].values():
            copy.wait_send()
    over.wait_send()

    def drain_piece(k, carry):
        deal(k).wait_send()
        return carry

    lax.fori_loop(1, DEPTHS, drain_piece, 0)


def migrate(extrap, source, record, shots, factor, angle_lag):
    vmem = pl.BlockSpec(memory_space=pltpu.VMEM)
    hbm = pl.BlockSpec(memory_space=pltpu.HBM)
    return pl.pallas_call(
        kernel,
        out_shape=jax.ShapeDtypeStruct((PIECE, DEPTHS, ANGLES), F32),
        in_specs=[hbm, hbm, hbm, hbm, pl.BlockSpec(memory_space=pltpu.SMEM), hbm],
        out_specs=vmem,
        scratch_shapes=[
            pltpu.VMEM((2, POINTS, POINTS), BF16),
            pltpu.VMEM((SHOTS, 2, POINTS), BF16),
            pltpu.VMEM((SHOTS, 2, POINTS), BF16),
            pltpu.VMEM((1, SHOTS), jnp.int32),
            pltpu.VMEM((POINTS, ANGLES), jnp.int32),
            pltpu.VMEM((BATCHES, 2 * HALF, POINTS), BF16),
            pltpu.VMEM((BATCHES, 2 * HALF, POINTS), BF16),
            pltpu.VMEM((2, 2 * SHOTS, POINTS), BF16),
            pltpu.VMEM((DEPTHS, POINTS, ANGLES), BF16),
            pltpu.VMEM((8, 2 * ROWS, POINTS), BF16),
            pltpu.VMEM((8, ROWS, POINTS), BF16),
            pltpu.VMEM((2, ROWS, POINTS), BF16),
            pltpu.VMEM((2, ROWS, POINTS), BF16),
            pltpu.VMEM((2, ROWS, POINTS), BF16),
            pltpu.VMEM((2, ROWS // 2, POINTS), BF16),
            pltpu.VMEM((2, ROWS // 2, POINTS), BF16),
            pltpu.VMEM((2, ROWS, POINTS), BF16),
            pltpu.VMEM((2, ROWS, POINTS), BF16),
            pltpu.VMEM((ROWS, POINTS), BF16),
            pltpu.VMEM((ROWS, POINTS), BF16),
            pltpu.VMEM((ROWS, POINTS), F32),
            pltpu.VMEM((DEPTHS, PIECE, POINTS), BF16),
            pltpu.VMEM((DEPTHS, PIECE, POINTS), BF16),
            pltpu.VMEM((ROWS, POINTS), F32),
            pltpu.VMEM((DEPTHS, 2, 2 * ROWS, LANES), F32),
            pltpu.SemaphoreType.DMA,
            pltpu.SemaphoreType.DMA,
            pltpu.SemaphoreType.DMA((3,)),
            pltpu.SemaphoreType.DMA((2 * BATCHES,)),
            pltpu.SemaphoreType.DMA((2 * BATCHES,)),
            pltpu.SemaphoreType.DMA((8,)),
            pltpu.SemaphoreType.DMA((8,)),
            pltpu.SemaphoreType.DMA((12,)),
            pltpu.SemaphoreType.DMA((12,)),
            pltpu.SemaphoreType.DMA,
            pltpu.SemaphoreType.DMA,
            pltpu.SemaphoreType.DMA((DEPTHS,)),
            pltpu.SemaphoreType.DMA((DEPTHS,)),
            pltpu.SemaphoreType.REGULAR,
        ],
        compiler_params=pltpu.CompilerParams(
            collective_id=0, has_side_effects=True, vmem_limit_bytes=67043328 - 200 * 1024
        ),
        name="migrate",
    )(extrap, source, record, shots, factor, angle_lag)


def shards(extrap, source_field, record_field, shot_of_record, freq_index, angle_lag):
    freq_count = lax.axis_size("freq")
    shots = shot_of_record.reshape(1, SHOTS)
    factor = (
        (freq_index.astype(F32) + 1.0) / (8 * freq_count) / math.sqrt(SHOTS * freq_count)
    )
    return migrate(
        extrap[0, 0], source_field[0], record_field[0], shots, factor, angle_lag
    )


def solution(mesh):
    placed = (
        P("depth", "freq", None, None, None),
        P("freq", None, None, None),
        P("freq", None, None, None),
        P(),
        P("freq"),
        P(),
    )
    return jax.shard_map(
        shards,
        mesh=mesh,
        in_specs=placed,
        out_specs=P(("freq", "depth"), None, None),
        check_vma=False,
    )
```

```python
import math

import jax
import jax.numpy as jnp
from jax import lax
from jax.experimental import pallas as pl
from jax.experimental.pallas import tpu as pltpu
from jax.sharding import PartitionSpec as P

MESH = pl.DeviceIdType.MESH
BATCH = 4
DEPTHS = 16
ROWS = 64
POINTS = 1024
ANGLES = 256
SHOTS = 128
LANES = 128
BATCHES = SHOTS // BATCH
HALF = 2 * BATCH
PIECE = ROWS // DEPTHS
ORDER = [(1, 2), (1, 1), (1, 3), (1, 0), (0, 2), (0, 1), (0, 3), (0, 0)]
F32 = jnp.float32
BF16 = jnp.bfloat16


def swap_parts(a, b):
    rolled = jnp.concatenate(
        [pltpu.roll(b[:HALF], BATCH, 0), pltpu.roll(b[HALF:], BATCH, 0)], axis=0
    )
    row = lax.broadcasted_iota(jnp.int32, rolled.shape, 0)
    minus = (row < BATCH) | (row >= HALF + BATCH)
    return a + jnp.where(minus, -rolled, rolled)


def expand(part):
    shape = (SHOTS, 2 * SHOTS)
    shot = lax.broadcasted_iota(jnp.int32, shape, 0)
    row = lax.broadcasted_iota(jnp.int32, shape, 1)
    hit = ((row // HALF) * BATCH + row % BATCH == shot) & ((row % HALF) // BATCH == part)
    return jnp.where(hit, 1.0, 0.0).astype(BF16)


def spread(shots, part):
    line = lax.broadcasted_iota(jnp.int32, (2 * SHOTS, SHOTS), 0)
    return jnp.where(2 * shots + part == line, 1.0, 0.0).astype(BF16)


def route(shots):
    total = jnp.dot(spread(shots, 0), expand(0), preferred_element_type=F32)
    total = total + jnp.dot(spread(shots, 1), expand(1), preferred_element_type=F32)
    return total.astype(BF16)


def kernel(
    e_hbm, source_hbm, record_hbm, shot_hbm, factor_ref, lag_hbm, out_ref,
    e_ref, source_ref, record_ref, shot_ref, lag_ref, inbuf, fin, field, sel, part, corein, two, one, three, rel_up, rel_down, from_down, from_up,
    ysend, yin, acc, pieces, gath, xs, g,
    e_sem, lag_sem, raw_sem, chain_send, chain_recv, core_send, core_recv, x_send, x_recv, y_send, y_recv, d_send, d_recv, greet_sem,
):
    d = lax.axis_index("depth")
    f = lax.axis_index("freq")
    core = f % 2
    x = (f // 2) % 4
    yh = f // 8
    partner = f + 1 - 2 * core
    up = yh * 8 + ((x + 1) % 4) * 2 + core
    down = yh * 8 + ((x + 3) % 4) * 2 + core
    across = f + 8 - 16 * yh

    load_e = pltpu.make_async_copy(e_hbm, e_ref, e_sem)
    load_lag = pltpu.make_async_copy(lag_hbm, lag_ref, lag_sem)
    raw = [
        pltpu.make_async_copy(shot_hbm, shot_ref, raw_sem.at[0]),
        pltpu.make_async_copy(source_hbm, source_ref, raw_sem.at[1]),
        pltpu.make_async_copy(record_hbm, record_ref, raw_sem.at[2]),
    ]

    @pl.when(d == 0)
    def _():
        for load in raw:
            load.start()

    load_e.start()
    load_lag.start()
    barrier = pltpu.get_barrier_semaphore()
    for other in (partner, up, down, across):
        pl.semaphore_signal(barrier, inc=1, device_id={"freq": other}, device_id_type=MESH)

    @pl.when(d > 0)
    def _():
        pl.semaphore_signal(barrier, inc=1, device_id={"depth": d - 1}, device_id_type=MESH)

    def build():
        load_lag.wait()

        def one_lag(lag, carry):
            sel[lag] = jnp.where(lag_ref[...] == lag, 1.0, 0.0).astype(BF16)
            g[lag, :, ROWS:, :] = jnp.zeros((2, ROWS, LANES), F32)
            return carry

        lax.fori_loop(0, DEPTHS, one_lag, 0)

    @pl.when(d > 0)
    def _():
        build()

    @pl.when(d == 0)
    def _():
        for load in raw:
            load.wait()
        straight = lax.broadcasted_iota(jnp.int32, (1, SHOTS), 1)
        packed = []
        for field_ref, shots in ((source_ref, shot_ref[...]), (record_ref, straight)):
            lines = field_ref[...].reshape(2 * SHOTS, POINTS)
            rows = lax.dot_general(
                route(shots), lines, (((0,), (0,)), ((), ())), preferred_element_type=F32
            )
            packed.append(rows.reshape(BATCHES, HALF, POINTS))
        inbuf[...] = jnp.concatenate(packed, axis=1).astype(BF16)

    load_e.wait()

    @pl.when(d < DEPTHS - 1)
    def _():
        pl.semaphore_wait(barrier, 5)

    @pl.when(d == DEPTHS - 1)
    def _():
        pl.semaphore_wait(barrier, 4)

    side = POINTS // 2
    sides = [slice(0, side), slice(side, POINTS)]

    def hop(b, n):
        columns = pl.ds(n * side, side)
        return pltpu.make_async_remote_copy(
            src_ref=fin.at[b, :, columns],
            dst_ref=inbuf.at[b, :, columns],
            send_sem=chain_send.at[2 * b + n],
            recv_sem=chain_recv.at[2 * b + n],
            device_id={"depth": d + 1},
            device_id_type=MESH,
        )

    def step(b):
        @pl.when(d > 0)
        def _():
            hop(b, 0).wait_recv()

        values = inbuf[b, :, sides[0]]
        first = jnp.dot(values, e_ref[0, sides[0], :], preferred_element_type=F32)
        second = jnp.dot(values, e_ref[1, sides[0], :], preferred_element_type=F32)

        @pl.when(d > 0)
        def _():
            hop(b, 1).wait_recv()

        values = inbuf[b, :, sides[1]]
        results = []
        for n in range(2):
            part_first = first[:, sides[n]] + jnp.dot(
                values, e_ref[0, sides[1], sides[n]], preferred_element_type=F32
            )
            part_second = second[:, sides[n]] + jnp.dot(
                values, e_ref[1, sides[1], sides[n]], preferred_element_type=F32
            )
            result = swap_parts(part_first, part_second)
            fin[b, :, sides[n]] = result.astype(BF16)

            @pl.when(d < DEPTHS - 1)
            def _():
                hop(b, n).start()

            results.append(result)
        return results

    def two_steps(p, carry):
        even = step(2 * p)
        odd = step(2 * p + 1)
        rows = pl.ds(pl.multiple_of(p * 2 * HALF, 2 * HALF), 2 * HALF)
        for n in range(2):
            field[0, rows, sides[n]] = jnp.concatenate(
                [even[n][:HALF], odd[n][:HALF]], axis=0
            ).astype(BF16)
            field[1, rows, sides[n]] = jnp.concatenate(
                [even[n][HALF:], odd[n][HALF:]], axis=0
            ).astype(BF16)
        return carry

    two_steps(0, 0)

    def greet(k, carry):
        pl.semaphore_signal(greet_sem, inc=1, device_id={"depth": k}, device_id_type=MESH)
        return carry

    lax.fori_loop(0, d, greet, 0)
    lax.fori_loop(1, BATCHES // 2, two_steps, 0)

    mine = pl.ds(pl.multiple_of(core * ROWS, ROWS), ROWS)
    theirs = pl.ds(pl.multiple_of((1 - core) * ROWS, ROWS), ROWS)

    def to_core(t):
        return pltpu.make_async_remote_copy(
            src_ref=part.at[t, theirs, :],
            dst_ref=corein.at[t],
            send_sem=core_send.at[t],
            recv_sem=core_recv.at[t],
            device_id={"freq": partner},
            device_id_type=MESH,
        )

    factor = factor_ref[0]
    for t, (q, r) in enumerate(ORDER):
        block = (yh + q * (1 - 2 * yh)) * 4 + (x + r) % 4
        columns = pl.ds(pl.multiple_of(block * 2 * ROWS, 2 * ROWS), 2 * ROWS)
        term = lax.dot_general(
            field[0, :, columns], field[1], (((0,), (0,)), ((), ())), preferred_element_type=F32
        )
        part[t] = (term * factor).astype(BF16)
        to_core(t).start()

    @pl.when(d == 0)
    def _():
        build()

    def pair(t, rows=slice(0, ROWS)):
        own = part[t, mine, :][rows]
        return own.astype(F32) + corein[t, rows, :].astype(F32)

    def ring(src, dst, s, target):
        return pltpu.make_async_remote_copy(
            src_ref=src,
            dst_ref=dst,
            send_sem=x_send.at[s],
            recv_sem=x_recv.at[s],
            device_id={"freq": target},
            device_id_type=MESH,
        )

    low, high = slice(0, ROWS // 2), slice(ROWS // 2, ROWS)
    copies = {}
    for q in (0, 1):
        base = 6 * q
        lo, hi = pl.ds(0, ROWS // 2), pl.ds(ROWS // 2, ROWS // 2)
        copies[q] = dict(
            two_up=ring(two.at[q, lo, :], rel_up.at[q], base, up),
            two_down=ring(two.at[q, hi, :], rel_down.at[q], base + 1, down),
            one_now=ring(one.at[q, hi, :], from_down.at[q, hi, :], base + 2, up),
            one_late=ring(one.at[q, lo, :], from_down.at[q, lo, :], base + 3, up),
            three_now=ring(three.at[q, lo, :], from_up.at[q, lo, :], base + 4, down),
            three_late=ring(three.at[q, hi, :], from_up.at[q, hi, :], base + 5, down),
        )

    def far(q):
        t = ORDER.index((q, 2))
        to_core(t).wait_recv()
        two[q] = pair(t).astype(BF16)
        copies[q]["two_up"].start()
        copies[q]["two_down"].start()

    def near(q):
        t = ORDER.index((q, 1))
        to_core(t).wait_recv()
        one[q] = pair(t).astype(BF16)
        copies[q]["one_now"].start()
        t = ORDER.index((q, 3))
        to_core(t).wait_recv()
        three[q] = pair(t).astype(BF16)
        copies[q]["three_now"].start()

    def relay(q):
        copies[q]["two_up"].wait_recv()
        one[q, low, :] = (one[q, low, :].astype(F32) + rel_up[q].astype(F32)).astype(BF16)
        copies[q]["one_late"].start()
        copies[q]["two_down"].wait_recv()
        three[q, high, :] = (three[q, high, :].astype(F32) + rel_down[q].astype(F32)).astype(BF16)
        copies[q]["three_late"].start()

    def collect(q):
        t = ORDER.index((q, 0))
        to_core(t).wait_recv()
        for name in ("one_now", "three_now", "one_late", "three_late"):
            copies[q][name].wait_recv()
        return pair(t) + from_down[q].astype(F32) + from_up[q].astype(F32)

    over = pltpu.make_async_remote_copy(
        src_ref=ysend, dst_ref=yin, send_sem=y_send, recv_sem=y_recv,
        device_id={"freq": across}, device_id_type=MESH,
    )
    far(1)
    near(1)
    far(0)
    relay(1)
    near(0)
    ysend[...] = collect(1).astype(BF16)
    over.start()
    relay(0)
    acc[...] = collect(0)
    over.wait_recv()
    acc[...] = acc[...] + yin[...].astype(F32)
    for k in range(DEPTHS):
        pieces[k] = acc[PIECE * k : PIECE * (k + 1), :].astype(BF16)

    def deal(k):
        target = (d + k) % DEPTHS
        return pltpu.make_async_remote_copy(
            src_ref=pieces.at[target],
            dst_ref=gath.at[d],
            send_sem=d_send.at[k],
            recv_sem=d_recv.at[k],
            device_id={"depth": target},
            device_id_type=MESH,
        )

    def arrival(k):
        source = (d + DEPTHS - k) % DEPTHS
        return pltpu.make_async_remote_copy(
            src_ref=pieces.at[source],
            dst_ref=gath.at[source],
            send_sem=d_send.at[k],
            recv_sem=d_recv.at[k],
            device_id={"depth": source},
            device_id_type=MESH,
        )

    def send_piece(k, carry):
        deal(k).start()
        return carry


    @pl.when(d < DEPTHS - 1)
    def _():
        pl.semaphore_wait(greet_sem, DEPTHS - 1 - d)

    lax.fori_loop(1, DEPTHS, send_piece, 0)
    gath[d] = pieces[d]

    def take_piece(k, carry):
        arrival(k).wait_recv()
        return carry

    lax.fori_loop(1, DEPTHS, take_piece, 0)
    for k in range(DEPTHS):
        xs[PIECE * k : PIECE * (k + 1), :] = gath[k].astype(F32)

    def stack(lag, carry):
        term = jnp.dot(xs[...].astype(BF16), sel[lag], preferred_element_type=F32)
        g[lag, 0, 0:ROWS, :] = term[:, :LANES]
        g[lag, 1, 0:ROWS, :] = term[:, LANES:]
        return carry

    lax.fori_loop(0, DEPTHS, stack, 0)
    scale = 1.0 / math.sqrt(POINTS)
    for row in range(PIECE):
        for wing in range(2):
            total = g[0, wing, pl.ds(row, DEPTHS, stride=PIECE), :]
            for lag in range(1, DEPTHS):
                total = total + g[lag, wing, pl.ds(PIECE * lag + row, DEPTHS, stride=PIECE), :]
            out_ref[row, :, LANES * wing : LANES * (wing + 1)] = total * scale

    @pl.when(d < DEPTHS - 1)
    def _():
        def drain(b, carry):
            hop(b, 0).wait_send()
            hop(b, 1).wait_send()
            return carry

        lax.fori_loop(0, BATCHES, drain, 0)

    for t in range(len(ORDER)):
        to_core(t).wait_send()
    for q in (0, 1):
        for copy in copies[q].values():
            copy.wait_send()
    over.wait_send()

    def drain_piece(k, carry):
        deal(k).wait_send()
        return carry

    lax.fori_loop(1, DEPTHS, drain_piece, 0)


def migrate(extrap, source, record, shots, factor, angle_lag):
    vmem = pl.BlockSpec(memory_space=pltpu.VMEM)
    hbm = pl.BlockSpec(memory_space=pltpu.HBM)
    return pl.pallas_call(
        kernel,
        out_shape=jax.ShapeDtypeStruct((PIECE, DEPTHS, ANGLES), F32),
        in_specs=[hbm, hbm, hbm, hbm, pl.BlockSpec(memory_space=pltpu.SMEM), hbm],
        out_specs=vmem,
        scratch_shapes=[
            pltpu.VMEM((2, POINTS, POINTS), BF16),
            pltpu.VMEM((SHOTS, 2, POINTS), BF16),
            pltpu.VMEM((SHOTS, 2, POINTS), BF16),
            pltpu.VMEM((1, SHOTS), jnp.int32),
            pltpu.VMEM((POINTS, ANGLES), jnp.int32),
            pltpu.VMEM((BATCHES, 2 * HALF, POINTS), BF16),
            pltpu.VMEM((BATCHES, 2 * HALF, POINTS), BF16),
            pltpu.VMEM((2, 2 * SHOTS, POINTS), BF16),
            pltpu.VMEM((DEPTHS, POINTS, ANGLES), BF16),
            pltpu.VMEM((8, 2 * ROWS, POINTS), BF16),
            pltpu.VMEM((8, ROWS, POINTS), BF16),
            pltpu.VMEM((2, ROWS, POINTS), BF16),
            pltpu.VMEM((2, ROWS, POINTS), BF16),
            pltpu.VMEM((2, ROWS, POINTS), BF16),
            pltpu.VMEM((2, ROWS // 2, POINTS), BF16),
            pltpu.VMEM((2, ROWS // 2, POINTS), BF16),
            pltpu.VMEM((2, ROWS, POINTS), BF16),
            pltpu.VMEM((2, ROWS, POINTS), BF16),
            pltpu.VMEM((ROWS, POINTS), BF16),
            pltpu.VMEM((ROWS, POINTS), BF16),
            pltpu.VMEM((ROWS, POINTS), F32),
            pltpu.VMEM((DEPTHS, PIECE, POINTS), BF16),
            pltpu.VMEM((DEPTHS, PIECE, POINTS), BF16),
            pltpu.VMEM((ROWS, POINTS), F32),
            pltpu.VMEM((DEPTHS, 2, 2 * ROWS, LANES), F32),
            pltpu.SemaphoreType.DMA,
            pltpu.SemaphoreType.DMA,
            pltpu.SemaphoreType.DMA((3,)),
            pltpu.SemaphoreType.DMA((2 * BATCHES,)),
            pltpu.SemaphoreType.DMA((2 * BATCHES,)),
            pltpu.SemaphoreType.DMA((8,)),
            pltpu.SemaphoreType.DMA((8,)),
            pltpu.SemaphoreType.DMA((12,)),
            pltpu.SemaphoreType.DMA((12,)),
            pltpu.SemaphoreType.DMA,
            pltpu.SemaphoreType.DMA,
            pltpu.SemaphoreType.DMA((DEPTHS,)),
            pltpu.SemaphoreType.DMA((DEPTHS,)),
            pltpu.SemaphoreType.REGULAR,
        ],
        compiler_params=pltpu.CompilerParams(
            collective_id=0, has_side_effects=True, vmem_limit_bytes=67043328 - 10400 * 1024
        ),
        name="migrate",
    )(extrap, source, record, shots, factor, angle_lag)


def shards(extrap, source_field, record_field, shot_of_record, freq_index, angle_lag):
    freq_count = lax.axis_size("freq")
    shots = shot_of_record.reshape(1, SHOTS)
    factor = (
        (freq_index.astype(F32) + 1.0) / (8 * freq_count) / math.sqrt(SHOTS * freq_count)
    )
    return migrate(
        extrap[0, 0], source_field[0], record_field[0], shots, factor, angle_lag
    )


def solution(mesh):
    placed = (
        P("depth", "freq", None, None, None),
        P("freq", None, None, None),
        P("freq", None, None, None),
        P(),
        P("freq"),
        P(),
    )
    return jax.shard_map(
        shards,
        mesh=mesh,
        in_specs=placed,
        out_specs=P(("freq", "depth"), None, None),
        check_vma=False,
    )
```

```python
import math

import jax
import jax.numpy as jnp
from jax import lax
from jax.experimental import pallas as pl
from jax.experimental.pallas import tpu as pltpu
from jax.sharding import PartitionSpec as P

MESH = pl.DeviceIdType.MESH
BATCH = 4
DEPTHS = 16
ROWS = 64
POINTS = 1024
ANGLES = 256
SHOTS = 128
LANES = 128
GROUP = 4
BATCHES = SHOTS // BATCH
HALF = 2 * BATCH
PIECE = ROWS // DEPTHS
ORDER = [(1, 2), (1, 1), (1, 3), (1, 0), (0, 2), (0, 1), (0, 3), (0, 0)]
F32 = jnp.float32
BF16 = jnp.bfloat16


def swap_parts(a, b):
    rolled = jnp.concatenate(
        [pltpu.roll(b[:HALF], BATCH, 0), pltpu.roll(b[HALF:], BATCH, 0)], axis=0
    )
    row = lax.broadcasted_iota(jnp.int32, rolled.shape, 0)
    minus = (row < BATCH) | (row >= HALF + BATCH)
    return a + jnp.where(minus, -rolled, rolled)


def expand(part):
    shape = (SHOTS, 2 * SHOTS)
    shot = lax.broadcasted_iota(jnp.int32, shape, 0)
    row = lax.broadcasted_iota(jnp.int32, shape, 1)
    hit = ((row // HALF) * BATCH + row % BATCH == shot) & ((row % HALF) // BATCH == part)
    return jnp.where(hit, 1.0, 0.0).astype(BF16)


def spread(shots, part):
    line = lax.broadcasted_iota(jnp.int32, (2 * SHOTS, SHOTS), 0)
    return jnp.where(2 * shots + part == line, 1.0, 0.0).astype(BF16)


def route(shots):
    total = jnp.dot(spread(shots, 0), expand(0), preferred_element_type=F32)
    total = total + jnp.dot(spread(shots, 1), expand(1), preferred_element_type=F32)
    return total.astype(BF16)


def kernel(
    e_hbm, source_hbm, record_hbm, shot_hbm, factor_ref, lag_hbm, out_ref,
    e_ref, source_ref, record_ref, shot_ref, lag_ref, inbuf, fin, field, sel, part, corein, two, one, three, rel_up, rel_down, from_down, from_up,
    ysend, yin, acc, pieces, gath, xs, xb, g,
    e_sem, lag_sem, raw_sem, chain_send, chain_recv, core_send, core_recv, x_send, x_recv, y_send, y_recv, d_send, d_recv, greet_sem,
):
    d = lax.axis_index("depth")
    f = lax.axis_index("freq")
    core = f % 2
    x = (f // 2) % 4
    yh = f // 8
    partner = f + 1 - 2 * core
    up = yh * 8 + ((x + 1) % 4) * 2 + core
    down = yh * 8 + ((x + 3) % 4) * 2 + core
    across = f + 8 - 16 * yh

    load_e = pltpu.make_async_copy(e_hbm, e_ref, e_sem)
    load_lag = pltpu.make_async_copy(lag_hbm, lag_ref, lag_sem)
    raw = [
        pltpu.make_async_copy(shot_hbm, shot_ref, raw_sem.at[0]),
        pltpu.make_async_copy(source_hbm, source_ref, raw_sem.at[1]),
        pltpu.make_async_copy(record_hbm, record_ref, raw_sem.at[2]),
    ]

    @pl.when(d == 0)
    def _():
        for load in raw:
            load.start()

    load_e.start()
    load_lag.start()
    barrier = pltpu.get_barrier_semaphore()
    for other in (partner, up, down, across):
        pl.semaphore_signal(barrier, inc=1, device_id={"freq": other}, device_id_type=MESH)

    @pl.when(d > 0)
    def _():
        pl.semaphore_signal(barrier, inc=1, device_id={"depth": d - 1}, device_id_type=MESH)

    def build():
        load_lag.wait()

        def one_lag(lag, carry):
            sel[lag] = jnp.where(lag_ref[...] == lag, 1.0, 0.0).astype(BF16)
            g[lag, :, ROWS:, :] = jnp.zeros((2, ROWS, LANES), F32)
            return carry

        lax.fori_loop(0, DEPTHS, one_lag, 0)

    @pl.when(d > 0)
    def _():
        build()

    @pl.when(d == 0)
    def _():
        for load in raw:
            load.wait()
        straight = lax.broadcasted_iota(jnp.int32, (1, SHOTS), 1)
        packed = []
        for field_ref, shots in ((source_ref, shot_ref[...]), (record_ref, straight)):
            lines = field_ref[...].reshape(2 * SHOTS, POINTS)
            rows = lax.dot_general(
                route(shots), lines, (((0,), (0,)), ((), ())), preferred_element_type=F32
            )
            packed.append(rows.reshape(BATCHES, HALF, POINTS))
        inbuf[...] = jnp.concatenate(packed, axis=1).astype(BF16)

    load_e.wait()

    @pl.when(d < DEPTHS - 1)
    def _():
        pl.semaphore_wait(barrier, 5)

    @pl.when(d == DEPTHS - 1)
    def _():
        pl.semaphore_wait(barrier, 4)

    side = POINTS // 2
    sides = [slice(0, side), slice(side, POINTS)]

    def hop(b, n):
        columns = pl.ds(n * side, side)
        return pltpu.make_async_remote_copy(
            src_ref=fin.at[b, :, columns],
            dst_ref=inbuf.at[b, :, columns],
            send_sem=chain_send.at[2 * b + n],
            recv_sem=chain_recv.at[2 * b + n],
            device_id={"depth": d + 1},
            device_id_type=MESH,
        )

    def step(b):
        @pl.when(d > 0)
        def _():
            hop(b, 0).wait_recv()

        values = inbuf[b, :, sides[0]]
        first = jnp.dot(values, e_ref[0, sides[0], :], preferred_element_type=F32)
        second = jnp.dot(values, e_ref[1, sides[0], :], preferred_element_type=F32)

        @pl.when(d > 0)
        def _():
            hop(b, 1).wait_recv()

        values = inbuf[b, :, sides[1]]
        results = []
        for n in range(2):
            part_first = first[:, sides[n]] + jnp.dot(
                values, e_ref[0, sides[1], sides[n]], preferred_element_type=F32
            )
            part_second = second[:, sides[n]] + jnp.dot(
                values, e_ref[1, sides[1], sides[n]], preferred_element_type=F32
            )
            result = swap_parts(part_first, part_second)
            fin[b, :, sides[n]] = result.astype(BF16)

            @pl.when(d < DEPTHS - 1)
            def _():
                hop(b, n).start()

            results.append(result)
        return results

    def two_steps(p, carry):
        even = step(2 * p)
        odd = step(2 * p + 1)
        rows = pl.ds(pl.multiple_of(p * 2 * HALF, 2 * HALF), 2 * HALF)
        for n in range(2):
            field[0, rows, sides[n]] = jnp.concatenate(
                [even[n][:HALF], odd[n][:HALF]], axis=0
            ).astype(BF16)
            field[1, rows, sides[n]] = jnp.concatenate(
                [even[n][HALF:], odd[n][HALF:]], axis=0
            ).astype(BF16)
        return carry

    two_steps(0, 0)

    def greet(k, carry):
        pl.semaphore_signal(greet_sem, inc=1, device_id={"depth": k}, device_id_type=MESH)
        return carry

    lax.fori_loop(0, d, greet, 0)
    lax.fori_loop(1, BATCHES // 2, two_steps, 0)

    mine = pl.ds(pl.multiple_of(core * ROWS, ROWS), ROWS)
    theirs = pl.ds(pl.multiple_of((1 - core) * ROWS, ROWS), ROWS)

    def to_core(t):
        return pltpu.make_async_remote_copy(
            src_ref=part.at[t, theirs, :],
            dst_ref=corein.at[t],
            send_sem=core_send.at[t],
            recv_sem=core_recv.at[t],
            device_id={"freq": partner},
            device_id_type=MESH,
        )

    factor = factor_ref[0]
    for t, (q, r) in enumerate(ORDER):
        block = (yh + q * (1 - 2 * yh)) * 4 + (x + r) % 4
        columns = pl.ds(pl.multiple_of(block * 2 * ROWS, 2 * ROWS), 2 * ROWS)
        term = lax.dot_general(
            field[0, :, columns], field[1], (((0,), (0,)), ((), ())), preferred_element_type=F32
        )
        part[t] = (term * factor).astype(BF16)
        to_core(t).start()

    @pl.when(d == 0)
    def _():
        build()

    def pair(t, rows=slice(0, ROWS)):
        own = part[t, mine, :][rows]
        return own.astype(F32) + corein[t, rows, :].astype(F32)

    def ring(src, dst, s, target):
        return pltpu.make_async_remote_copy(
            src_ref=src,
            dst_ref=dst,
            send_sem=x_send.at[s],
            recv_sem=x_recv.at[s],
            device_id={"freq": target},
            device_id_type=MESH,
        )

    low, high = slice(0, ROWS // 2), slice(ROWS // 2, ROWS)
    copies = {}
    for q in (0, 1):
        base = 6 * q
        lo, hi = pl.ds(0, ROWS // 2), pl.ds(ROWS // 2, ROWS // 2)
        copies[q] = dict(
            two_up=ring(two.at[q, lo, :], rel_up.at[q], base, up),
            two_down=ring(two.at[q, hi, :], rel_down.at[q], base + 1, down),
            one_now=ring(one.at[q, hi, :], from_down.at[q, hi, :], base + 2, up),
            one_late=ring(one.at[q, lo, :], from_down.at[q, lo, :], base + 3, up),
            three_now=ring(three.at[q, lo, :], from_up.at[q, lo, :], base + 4, down),
            three_late=ring(three.at[q, hi, :], from_up.at[q, hi, :], base + 5, down),
        )

    def far(q):
        t = ORDER.index((q, 2))
        to_core(t).wait_recv()
        two[q] = pair(t).astype(BF16)
        copies[q]["two_up"].start()
        copies[q]["two_down"].start()

    def near(q):
        t = ORDER.index((q, 1))
        to_core(t).wait_recv()
        one[q] = pair(t).astype(BF16)
        copies[q]["one_now"].start()
        t = ORDER.index((q, 3))
        to_core(t).wait_recv()
        three[q] = pair(t).astype(BF16)
        copies[q]["three_now"].start()

    def relay(q):
        copies[q]["two_up"].wait_recv()
        one[q, low, :] = (one[q, low, :].astype(F32) + rel_up[q].astype(F32)).astype(BF16)
        copies[q]["one_late"].start()
        copies[q]["two_down"].wait_recv()
        three[q, high, :] = (three[q, high, :].astype(F32) + rel_down[q].astype(F32)).astype(BF16)
        copies[q]["three_late"].start()

    def collect(q):
        t = ORDER.index((q, 0))
        to_core(t).wait_recv()
        for name in ("one_now", "three_now", "one_late", "three_late"):
            copies[q][name].wait_recv()
        return pair(t) + from_down[q].astype(F32) + from_up[q].astype(F32)

    over = pltpu.make_async_remote_copy(
        src_ref=ysend, dst_ref=yin, send_sem=y_send, recv_sem=y_recv,
        device_id={"freq": across}, device_id_type=MESH,
    )
    far(1)
    near(1)
    far(0)
    relay(1)
    near(0)
    ysend[...] = collect(1).astype(BF16)
    over.start()
    relay(0)
    acc[...] = collect(0)
    over.wait_recv()
    acc[...] = acc[...] + yin[...].astype(F32)
    for k in range(DEPTHS):
        pieces[k] = acc[PIECE * k : PIECE * (k + 1), :].astype(BF16)

    def deal(k):
        target = (d + k) % DEPTHS
        return pltpu.make_async_remote_copy(
            src_ref=pieces.at[target],
            dst_ref=gath.at[d],
            send_sem=d_send.at[k],
            recv_sem=d_recv.at[k],
            device_id={"depth": target},
            device_id_type=MESH,
        )

    def arrival(k):
        source = (d + DEPTHS - k) % DEPTHS
        return pltpu.make_async_remote_copy(
            src_ref=pieces.at[source],
            dst_ref=gath.at[source],
            send_sem=d_send.at[k],
            recv_sem=d_recv.at[k],
            device_id={"depth": source},
            device_id_type=MESH,
        )

    def send_piece(k, carry):
        deal(k).start()
        return carry


    @pl.when(d < DEPTHS - 1)
    def _():
        pl.semaphore_wait(greet_sem, DEPTHS - 1 - d)

    lax.fori_loop(1, DEPTHS, send_piece, 0)
    gath[d] = pieces[d]

    def take_piece(k, carry):
        arrival(k).wait_recv()
        return carry

    lax.fori_loop(1, DEPTHS, take_piece, 0)
    for k in range(DEPTHS):
        xs[PIECE * k : PIECE * (k + 1), :] = gath[k].astype(F32)

    xb[...] = xs[...].astype(BF16)

    def stack(p, carry):
        lags = [GROUP * p + k for k in range(GROUP)]
        terms = [jnp.dot(xb[...], sel[lag], preferred_element_type=F32) for lag in lags]
        for lag, term in zip(lags, terms):
            g[lag, 0, 0:ROWS, :] = term[:, :LANES]
            g[lag, 1, 0:ROWS, :] = term[:, LANES:]
        return carry

    lax.fori_loop(0, DEPTHS // GROUP, stack, 0)
    scale = 1.0 / math.sqrt(POINTS)
    for row in range(PIECE):
        for wing in range(2):
            total = g[0, wing, pl.ds(row, DEPTHS, stride=PIECE), :]
            for lag in range(1, DEPTHS):
                total = total + g[lag, wing, pl.ds(PIECE * lag + row, DEPTHS, stride=PIECE), :]
            out_ref[row, :, LANES * wing : LANES * (wing + 1)] = total * scale

    @pl.when(d < DEPTHS - 1)
    def _():
        def drain(b, carry):
            hop(b, 0).wait_send()
            hop(b, 1).wait_send()
            return carry

        lax.fori_loop(0, BATCHES, drain, 0)

    for t in range(len(ORDER)):
        to_core(t).wait_send()
    for q in (0, 1):
        for copy in copies[q].values():
            copy.wait_send()
    over.wait_send()

    def drain_piece(k, carry):
        deal(k).wait_send()
        return carry

    lax.fori_loop(1, DEPTHS, drain_piece, 0)


def migrate(extrap, source, record, shots, factor, angle_lag):
    vmem = pl.BlockSpec(memory_space=pltpu.VMEM)
    hbm = pl.BlockSpec(memory_space=pltpu.HBM)
    return pl.pallas_call(
        kernel,
        out_shape=jax.ShapeDtypeStruct((PIECE, DEPTHS, ANGLES), F32),
        in_specs=[hbm, hbm, hbm, hbm, pl.BlockSpec(memory_space=pltpu.SMEM), hbm],
        out_specs=vmem,
        scratch_shapes=[
            pltpu.VMEM((2, POINTS, POINTS), BF16),
            pltpu.VMEM((SHOTS, 2, POINTS), BF16),
            pltpu.VMEM((SHOTS, 2, POINTS), BF16),
            pltpu.VMEM((1, SHOTS), jnp.int32),
            pltpu.VMEM((POINTS, ANGLES), jnp.int32),
            pltpu.VMEM((BATCHES, 2 * HALF, POINTS), BF16),
            pltpu.VMEM((BATCHES, 2 * HALF, POINTS), BF16),
            pltpu.VMEM((2, 2 * SHOTS, POINTS), BF16),
            pltpu.VMEM((DEPTHS, POINTS, ANGLES), BF16),
            pltpu.VMEM((8, 2 * ROWS, POINTS), BF16),
            pltpu.VMEM((8, ROWS, POINTS), BF16),
            pltpu.VMEM((2, ROWS, POINTS), BF16),
            pltpu.VMEM((2, ROWS, POINTS), BF16),
            pltpu.VMEM((2, ROWS, POINTS), BF16),
            pltpu.VMEM((2, ROWS // 2, POINTS), BF16),
            pltpu.VMEM((2, ROWS // 2, POINTS), BF16),
            pltpu.VMEM((2, ROWS, POINTS), BF16),
            pltpu.VMEM((2, ROWS, POINTS), BF16),
            pltpu.VMEM((ROWS, POINTS), BF16),
            pltpu.VMEM((ROWS, POINTS), BF16),
            pltpu.VMEM((ROWS, POINTS), F32),
            pltpu.VMEM((DEPTHS, PIECE, POINTS), BF16),
            pltpu.VMEM((DEPTHS, PIECE, POINTS), BF16),
            pltpu.VMEM((ROWS, POINTS), F32),
            pltpu.VMEM((ROWS, POINTS), BF16),
            pltpu.VMEM((DEPTHS, 2, 2 * ROWS, LANES), F32),
            pltpu.SemaphoreType.DMA,
            pltpu.SemaphoreType.DMA,
            pltpu.SemaphoreType.DMA((3,)),
            pltpu.SemaphoreType.DMA((2 * BATCHES,)),
            pltpu.SemaphoreType.DMA((2 * BATCHES,)),
            pltpu.SemaphoreType.DMA((8,)),
            pltpu.SemaphoreType.DMA((8,)),
            pltpu.SemaphoreType.DMA((12,)),
            pltpu.SemaphoreType.DMA((12,)),
            pltpu.SemaphoreType.DMA,
            pltpu.SemaphoreType.DMA,
            pltpu.SemaphoreType.DMA((DEPTHS,)),
            pltpu.SemaphoreType.DMA((DEPTHS,)),
            pltpu.SemaphoreType.REGULAR,
        ],
        compiler_params=pltpu.CompilerParams(
            collective_id=0, has_side_effects=True, vmem_limit_bytes=67043328 - 10400 * 1024
        ),
        name="migrate",
    )(extrap, source, record, shots, factor, angle_lag)


def shards(extrap, source_field, record_field, shot_of_record, freq_index, angle_lag):
    freq_count = lax.axis_size("freq")
    shots = shot_of_record.reshape(1, SHOTS)
    factor = (
        (freq_index.astype(F32) + 1.0) / (8 * freq_count) / math.sqrt(SHOTS * freq_count)
    )
    return migrate(
        extrap[0, 0], source_field[0], record_field[0], shots, factor, angle_lag
    )


def solution(mesh):
    placed = (
        P("depth", "freq", None, None, None),
        P("freq", None, None, None),
        P("freq", None, None, None),
        P(),
        P("freq"),
        P(),
    )
    return jax.shard_map(
        shards,
        mesh=mesh,
        in_specs=placed,
        out_specs=P(("freq", "depth"), None, None),
        check_vma=False,
    )
```

```python
import math

import jax
import jax.numpy as jnp
from jax import lax
from jax.experimental import pallas as pl
from jax.experimental.pallas import tpu as pltpu
from jax.sharding import PartitionSpec as P

MESH = pl.DeviceIdType.MESH
BATCH = 4
DEPTHS = 16
ROWS = 64
POINTS = 1024
ANGLES = 256
SHOTS = 128
LANES = 128
GROUP = 4
BATCHES = SHOTS // BATCH
HALF = 2 * BATCH
PIECE = ROWS // DEPTHS
ORDER = [(1, 2), (1, 1), (1, 3), (1, 0), (0, 2), (0, 1), (0, 3), (0, 0)]
F32 = jnp.float32
BF16 = jnp.bfloat16


def swap_parts(a, b):
    rolled = jnp.concatenate(
        [pltpu.roll(b[:HALF], BATCH, 0), pltpu.roll(b[HALF:], BATCH, 0)], axis=0
    )
    row = lax.broadcasted_iota(jnp.int32, rolled.shape, 0)
    minus = (row < BATCH) | (row >= HALF + BATCH)
    return a + jnp.where(minus, -rolled, rolled)


def expand(part):
    shape = (SHOTS, 2 * SHOTS)
    shot = lax.broadcasted_iota(jnp.int32, shape, 0)
    row = lax.broadcasted_iota(jnp.int32, shape, 1)
    hit = ((row // HALF) * BATCH + row % BATCH == shot) & ((row % HALF) // BATCH == part)
    return jnp.where(hit, 1.0, 0.0).astype(BF16)


def spread(shots, part):
    line = lax.broadcasted_iota(jnp.int32, (2 * SHOTS, SHOTS), 0)
    return jnp.where(2 * shots + part == line, 1.0, 0.0).astype(BF16)


def route(shots):
    total = jnp.dot(spread(shots, 0), expand(0), preferred_element_type=F32)
    total = total + jnp.dot(spread(shots, 1), expand(1), preferred_element_type=F32)
    return total.astype(BF16)


def kernel(
    e_hbm, source_hbm, record_hbm, shot_hbm, factor_ref, lag_hbm, out_ref,
    e_ref, source_ref, record_ref, shot_ref, lag_ref, inbuf, fin, field, sel, part, corein, two, one, three, rel_up, rel_down, from_down, from_up,
    acc, pieces, gath, xs, xb, g,
    e_sem, lag_sem, raw_sem, chain_send, chain_recv, core_send, core_recv, x_send, x_recv, d_send, d_recv, greet_sem,
):
    d = lax.axis_index("depth")
    f = lax.axis_index("freq")
    core = f % 2
    x = (f // 2) % 4
    yh = f // 8
    partner = f + 1 - 2 * core
    up = yh * 8 + ((x + 1) % 4) * 2 + core
    down = yh * 8 + ((x + 3) % 4) * 2 + core
    across = f + 8 - 16 * yh

    side = POINTS // 2
    sides = [slice(0, side), slice(side, POINTS)]
    load_e = [
        pltpu.make_async_copy(
            e_hbm.at[:, pl.ds(n * side, side), :], e_ref.at[:, pl.ds(n * side, side), :], e_sem.at[n]
        )
        for n in range(2)
    ]
    load_lag = pltpu.make_async_copy(lag_hbm, lag_ref, lag_sem)
    raw = [
        pltpu.make_async_copy(shot_hbm, shot_ref, raw_sem.at[0]),
        pltpu.make_async_copy(source_hbm, source_ref, raw_sem.at[1]),
        pltpu.make_async_copy(record_hbm, record_ref, raw_sem.at[2]),
    ]

    @pl.when(d == 0)
    def _():
        for load in raw:
            load.start()

    for load in load_e:
        load.start()
    load_lag.start()
    barrier = pltpu.get_barrier_semaphore()
    for other in (partner, up, down, across):
        pl.semaphore_signal(barrier, inc=1, device_id={"freq": other}, device_id_type=MESH)

    @pl.when(d > 0)
    def _():
        pl.semaphore_signal(barrier, inc=1, device_id={"depth": d - 1}, device_id_type=MESH)

    def build():
        load_lag.wait()

        def one_lag(lag, carry):
            sel[lag] = jnp.where(lag_ref[...] == lag, 1.0, 0.0).astype(BF16)
            g[lag, :, ROWS:, :] = jnp.zeros((2, ROWS, LANES), F32)
            return carry

        lax.fori_loop(0, DEPTHS, one_lag, 0)

    @pl.when(d > 0)
    def _():
        build()

    @pl.when(d == 0)
    def _():
        for load in raw:
            load.wait()
        straight = lax.broadcasted_iota(jnp.int32, (1, SHOTS), 1)
        packed = []
        for field_ref, shots in ((source_ref, shot_ref[...]), (record_ref, straight)):
            lines = field_ref[...].reshape(2 * SHOTS, POINTS)
            rows = lax.dot_general(
                route(shots), lines, (((0,), (0,)), ((), ())), preferred_element_type=F32
            )
            packed.append(rows.reshape(BATCHES, HALF, POINTS))
        inbuf[...] = jnp.concatenate(packed, axis=1).astype(BF16)

    @pl.when(d < DEPTHS - 1)
    def _():
        pl.semaphore_wait(barrier, 5)

    @pl.when(d == DEPTHS - 1)
    def _():
        pl.semaphore_wait(barrier, 4)

    def hop(b, n):
        columns = pl.ds(n * side, side)
        return pltpu.make_async_remote_copy(
            src_ref=fin.at[b, :, columns],
            dst_ref=inbuf.at[b, :, columns],
            send_sem=chain_send.at[2 * b + n],
            recv_sem=chain_recv.at[2 * b + n],
            device_id={"depth": d + 1},
            device_id_type=MESH,
        )

    def step(b, first_step=False):
        if first_step:
            load_e[0].wait()

        @pl.when(d > 0)
        def _():
            hop(b, 0).wait_recv()

        values = inbuf[b, :, sides[0]]
        first = jnp.dot(values, e_ref[0, sides[0], :], preferred_element_type=F32)
        second = jnp.dot(values, e_ref[1, sides[0], :], preferred_element_type=F32)

        @pl.when(d > 0)
        def _():
            hop(b, 1).wait_recv()

        if first_step:
            load_e[1].wait()
        values = inbuf[b, :, sides[1]]
        results = []
        for n in range(2):
            part_first = first[:, sides[n]] + jnp.dot(
                values, e_ref[0, sides[1], sides[n]], preferred_element_type=F32
            )
            part_second = second[:, sides[n]] + jnp.dot(
                values, e_ref[1, sides[1], sides[n]], preferred_element_type=F32
            )
            result = swap_parts(part_first, part_second)
            fin[b, :, sides[n]] = result.astype(BF16)

            @pl.when(d < DEPTHS - 1)
            def _():
                hop(b, n).start()

            results.append(result)
        return results

    def two_steps(p, carry, first_step=False):
        even = step(2 * p, first_step)
        odd = step(2 * p + 1)
        rows = pl.ds(pl.multiple_of(p * 2 * HALF, 2 * HALF), 2 * HALF)
        for n in range(2):
            field[0, rows, sides[n]] = jnp.concatenate(
                [even[n][:HALF], odd[n][:HALF]], axis=0
            ).astype(BF16)
            field[1, rows, sides[n]] = jnp.concatenate(
                [even[n][HALF:], odd[n][HALF:]], axis=0
            ).astype(BF16)
        return carry

    two_steps(0, 0, True)

    def greet(k, carry):
        for peer in (f, across):
            pl.semaphore_signal(
                greet_sem, inc=1, device_id={"depth": k, "freq": peer}, device_id_type=MESH
            )
        return carry

    lax.fori_loop(0, d, greet, 0)
    lax.fori_loop(1, BATCHES // 2, two_steps, 0)

    mine = pl.ds(pl.multiple_of(core * ROWS, ROWS), ROWS)
    theirs = pl.ds(pl.multiple_of((1 - core) * ROWS, ROWS), ROWS)

    def to_core(t):
        return pltpu.make_async_remote_copy(
            src_ref=part.at[t, theirs, :],
            dst_ref=corein.at[t],
            send_sem=core_send.at[t],
            recv_sem=core_recv.at[t],
            device_id={"freq": partner},
            device_id_type=MESH,
        )

    factor = factor_ref[0]
    for pair_start in range(0, len(ORDER), 2):
        for t in (pair_start, pair_start + 1):
            q, r = ORDER[t]
            block = (yh + q * (1 - 2 * yh)) * 4 + (x + r) % 4
            columns = pl.ds(pl.multiple_of(block * 2 * ROWS, 2 * ROWS), 2 * ROWS)
            term = lax.dot_general(
                field[0, :, columns], field[1], (((0,), (0,)), ((), ())), preferred_element_type=F32
            )
            part[t] = (term * factor).astype(BF16)
        to_core(pair_start).start()
        to_core(pair_start + 1).start()

    @pl.when(d == 0)
    def _():
        build()

    def pair(t, rows=slice(0, ROWS)):
        own = part[t, mine, :][rows]
        return own.astype(F32) + corein[t, rows, :].astype(F32)

    def ring(src, dst, s, target):
        return pltpu.make_async_remote_copy(
            src_ref=src,
            dst_ref=dst,
            send_sem=x_send.at[s],
            recv_sem=x_recv.at[s],
            device_id={"freq": target},
            device_id_type=MESH,
        )

    low, high = slice(0, ROWS // 2), slice(ROWS // 2, ROWS)
    copies = {}
    for q in (0, 1):
        base = 6 * q
        lo, hi = pl.ds(0, ROWS // 2), pl.ds(ROWS // 2, ROWS // 2)
        copies[q] = dict(
            two_up=ring(two.at[q, lo, :], rel_up.at[q], base, up),
            two_down=ring(two.at[q, hi, :], rel_down.at[q], base + 1, down),
            one_now=ring(one.at[q, hi, :], from_down.at[q, hi, :], base + 2, up),
            one_late=ring(one.at[q, lo, :], from_down.at[q, lo, :], base + 3, up),
            three_now=ring(three.at[q, lo, :], from_up.at[q, lo, :], base + 4, down),
            three_late=ring(three.at[q, hi, :], from_up.at[q, hi, :], base + 5, down),
        )

    def far(q):
        t = ORDER.index((q, 2))
        to_core(t).wait_recv()
        two[q] = pair(t).astype(BF16)
        copies[q]["two_up"].start()
        copies[q]["two_down"].start()

    def near(q):
        t = ORDER.index((q, 1))
        to_core(t).wait_recv()
        one[q] = pair(t).astype(BF16)
        copies[q]["one_now"].start()
        t = ORDER.index((q, 3))
        to_core(t).wait_recv()
        three[q] = pair(t).astype(BF16)
        copies[q]["three_now"].start()

    def relay(q):
        copies[q]["two_up"].wait_recv()
        one[q, low, :] = (one[q, low, :].astype(F32) + rel_up[q].astype(F32)).astype(BF16)
        copies[q]["one_late"].start()
        copies[q]["two_down"].wait_recv()
        three[q, high, :] = (three[q, high, :].astype(F32) + rel_down[q].astype(F32)).astype(BF16)
        copies[q]["three_late"].start()

    def collect(q):
        t = ORDER.index((q, 0))
        to_core(t).wait_recv()
        for name in ("one_now", "three_now", "one_late", "three_late"):
            copies[q][name].wait_recv()
        return pair(t) + from_down[q].astype(F32) + from_up[q].astype(F32)

    far(1)
    near(1)
    far(0)
    relay(1)
    near(0)
    relay(0)

    def deal(q, k):
        target = (d + k) % DEPTHS
        return pltpu.make_async_remote_copy(
            src_ref=pieces.at[q, target],
            dst_ref=gath.at[q, d],
            send_sem=d_send.at[q, k],
            recv_sem=d_recv.at[q, k],
            device_id={"depth": target, "freq": across if q else f},
            device_id_type=MESH,
        )

    def arrival(q, k):
        source = (d + DEPTHS - k) % DEPTHS
        return pltpu.make_async_remote_copy(
            src_ref=pieces.at[q, source],
            dst_ref=gath.at[q, source],
            send_sem=d_send.at[q, k],
            recv_sem=d_recv.at[q, k],
            device_id={"depth": source, "freq": across if q else f},
            device_id_type=MESH,
        )

    for q in (1, 0):
        acc[...] = collect(q)
        for k in range(DEPTHS):
            pieces[q, k] = acc[PIECE * k : PIECE * (k + 1), :].astype(BF16)
        if q:
            @pl.when(d < DEPTHS - 1)
            def _():
                pl.semaphore_wait(greet_sem, 2 * (DEPTHS - 1 - d))

        def send_piece(i, carry):
            deal(q, DEPTHS // 2 + (i // 2 + i % 2) * (1 - 2 * (i % 2))).start()
            return carry

        lax.fori_loop(0, DEPTHS - 1, send_piece, 0)
        if q:
            deal(q, 0).start()
    gath[0, d] = pieces[0, d]

    for q in (1, 0):
        def take_piece(k, carry):
            arrival(q, k).wait_recv()
            return carry

        lax.fori_loop(1 - q, DEPTHS, take_piece, 0)
    for k in range(DEPTHS):
        xs[PIECE * k : PIECE * (k + 1), :] = gath[0, k].astype(F32) + gath[1, k].astype(F32)

    xb[...] = xs[...].astype(BF16)

    def stack(p, carry):
        lags = [GROUP * p + k for k in range(GROUP)]
        terms = [jnp.dot(xb[...], sel[lag], preferred_element_type=F32) for lag in lags]
        for lag, term in zip(lags, terms):
            g[lag, 0, 0:ROWS, :] = term[:, :LANES]
            g[lag, 1, 0:ROWS, :] = term[:, LANES:]
        return carry

    lax.fori_loop(0, DEPTHS // GROUP, stack, 0)
    scale = 1.0 / math.sqrt(POINTS)
    for row in range(PIECE):
        for wing in range(2):
            total = g[0, wing, pl.ds(row, DEPTHS, stride=PIECE), :]
            for lag in range(1, DEPTHS):
                total = total + g[lag, wing, pl.ds(PIECE * lag + row, DEPTHS, stride=PIECE), :]
            out_ref[row, :, LANES * wing : LANES * (wing + 1)] = total * scale

    @pl.when(d < DEPTHS - 1)
    def _():
        def drain(b, carry):
            hop(b, 0).wait_send()
            hop(b, 1).wait_send()
            return carry

        lax.fori_loop(0, BATCHES, drain, 0)

    for t in range(len(ORDER)):
        to_core(t).wait_send()
    for q in (0, 1):
        for copy in copies[q].values():
            copy.wait_send()
    for q in (1, 0):
        def drain_piece(k, carry):
            deal(q, k).wait_send()
            return carry

        lax.fori_loop(1 - q, DEPTHS, drain_piece, 0)


def migrate(extrap, source, record, shots, factor, angle_lag):
    vmem = pl.BlockSpec(memory_space=pltpu.VMEM)
    hbm = pl.BlockSpec(memory_space=pltpu.HBM)
    return pl.pallas_call(
        kernel,
        out_shape=jax.ShapeDtypeStruct((PIECE, DEPTHS, ANGLES), F32),
        in_specs=[hbm, hbm, hbm, hbm, pl.BlockSpec(memory_space=pltpu.SMEM), hbm],
        out_specs=vmem,
        scratch_shapes=[
            pltpu.VMEM((2, POINTS, POINTS), BF16),
            pltpu.VMEM((SHOTS, 2, POINTS), BF16),
            pltpu.VMEM((SHOTS, 2, POINTS), BF16),
            pltpu.VMEM((1, SHOTS), jnp.int32),
            pltpu.VMEM((POINTS, ANGLES), jnp.int32),
            pltpu.VMEM((BATCHES, 2 * HALF, POINTS), BF16),
            pltpu.VMEM((BATCHES, 2 * HALF, POINTS), BF16),
            pltpu.VMEM((2, 2 * SHOTS, POINTS), BF16),
            pltpu.VMEM((DEPTHS, POINTS, ANGLES), BF16),
            pltpu.VMEM((8, 2 * ROWS, POINTS), BF16),
            pltpu.VMEM((8, ROWS, POINTS), BF16),
            pltpu.VMEM((2, ROWS, POINTS), BF16),
            pltpu.VMEM((2, ROWS, POINTS), BF16),
            pltpu.VMEM((2, ROWS, POINTS), BF16),
            pltpu.VMEM((2, ROWS // 2, POINTS), BF16),
            pltpu.VMEM((2, ROWS // 2, POINTS), BF16),
            pltpu.VMEM((2, ROWS, POINTS), BF16),
            pltpu.VMEM((2, ROWS, POINTS), BF16),
            pltpu.VMEM((ROWS, POINTS), F32),
            pltpu.VMEM((2, DEPTHS, PIECE, POINTS), BF16),
            pltpu.VMEM((2, DEPTHS, PIECE, POINTS), BF16),
            pltpu.VMEM((ROWS, POINTS), F32),
            pltpu.VMEM((ROWS, POINTS), BF16),
            pltpu.VMEM((DEPTHS, 2, 2 * ROWS, LANES), F32),
            pltpu.SemaphoreType.DMA((2,)),
            pltpu.SemaphoreType.DMA,
            pltpu.SemaphoreType.DMA((3,)),
            pltpu.SemaphoreType.DMA((2 * BATCHES,)),
            pltpu.SemaphoreType.DMA((2 * BATCHES,)),
            pltpu.SemaphoreType.DMA((8,)),
            pltpu.SemaphoreType.DMA((8,)),
            pltpu.SemaphoreType.DMA((12,)),
            pltpu.SemaphoreType.DMA((12,)),
            pltpu.SemaphoreType.DMA((2, DEPTHS)),
            pltpu.SemaphoreType.DMA((2, DEPTHS)),
            pltpu.SemaphoreType.REGULAR,
        ],
        compiler_params=pltpu.CompilerParams(
            collective_id=0, has_side_effects=True, vmem_limit_bytes=67043328 - 10400 * 1024
        ),
        name="migrate",
    )(extrap, source, record, shots, factor, angle_lag)


def shards(extrap, source_field, record_field, shot_of_record, freq_index, angle_lag):
    freq_count = lax.axis_size("freq")
    shots = shot_of_record.reshape(1, SHOTS)
    factor = (
        (freq_index.astype(F32) + 1.0) / (8 * freq_count) / math.sqrt(SHOTS * freq_count)
    )
    return migrate(
        extrap[0, 0], source_field[0], record_field[0], shots, factor, angle_lag
    )


def solution(mesh):
    placed = (
        P("depth", "freq", None, None, None),
        P("freq", None, None, None),
        P("freq", None, None, None),
        P(),
        P("freq"),
        P(),
    )
    return jax.shard_map(
        shards,
        mesh=mesh,
        in_specs=placed,
        out_specs=P(("freq", "depth"), None, None),
        check_vma=False,
    )
```

```python
import math

import jax
import jax.numpy as jnp
from jax import lax
from jax.experimental import pallas as pl
from jax.experimental.pallas import tpu as pltpu
from jax.sharding import PartitionSpec as P

MESH = pl.DeviceIdType.MESH
BATCH = 4
DEPTHS = 16
ROWS = 64
POINTS = 1024
ANGLES = 256
SHOTS = 128
LANES = 128
GROUP = 4
BATCHES = SHOTS // BATCH
HALF = 2 * BATCH
PIECE = ROWS // DEPTHS
ORDER = [(1, 2), (1, 1), (1, 3), (1, 0), (0, 2), (0, 1), (0, 3), (0, 0)]
F32 = jnp.float32
BF16 = jnp.bfloat16


def swap_parts(a, b):
    rolled = jnp.concatenate(
        [pltpu.roll(b[:HALF], BATCH, 0), pltpu.roll(b[HALF:], BATCH, 0)], axis=0
    )
    row = lax.broadcasted_iota(jnp.int32, rolled.shape, 0)
    minus = (row < BATCH) | (row >= HALF + BATCH)
    return a + jnp.where(minus, -rolled, rolled)


def expand(part):
    shape = (SHOTS, 2 * SHOTS)
    shot = lax.broadcasted_iota(jnp.int32, shape, 0)
    row = lax.broadcasted_iota(jnp.int32, shape, 1)
    hit = ((row // HALF) * BATCH + row % BATCH == shot) & ((row % HALF) // BATCH == part)
    return jnp.where(hit, 1.0, 0.0).astype(BF16)


def spread(shots, part):
    line = lax.broadcasted_iota(jnp.int32, (2 * SHOTS, SHOTS), 0)
    return jnp.where(2 * shots + part == line, 1.0, 0.0).astype(BF16)


def route(shots):
    total = jnp.dot(spread(shots, 0), expand(0), preferred_element_type=F32)
    total = total + jnp.dot(spread(shots, 1), expand(1), preferred_element_type=F32)
    return total.astype(BF16)


def kernel(
    e_hbm, source_hbm, record_hbm, shot_hbm, factor_ref, lag_hbm, out_ref,
    e_ref, source_ref, record_ref, shot_ref, lag_ref, inbuf, fin, field, sel, part, corein, two, one, three, rel_up, rel_down, from_down, from_up,
    acc, pieces, gath, xs, xb, g,
    e_sem, lag_sem, raw_sem, chain_send, chain_recv, core_send, core_recv, x_send, x_recv, d_send, d_recv, greet_sem, token_sem,
):
    d = lax.axis_index("depth")
    f = lax.axis_index("freq")
    core = f % 2
    x = (f // 2) % 4
    yh = f // 8
    partner = f + 1 - 2 * core
    up = yh * 8 + ((x + 1) % 4) * 2 + core
    down = yh * 8 + ((x + 3) % 4) * 2 + core
    across = f + 8 - 16 * yh

    side = POINTS // 2
    sides = [slice(0, side), slice(side, POINTS)]
    load_e = [
        pltpu.make_async_copy(
            e_hbm.at[:, pl.ds(n * side, side), :], e_ref.at[:, pl.ds(n * side, side), :], e_sem.at[n]
        )
        for n in range(2)
    ]
    load_lag = pltpu.make_async_copy(lag_hbm, lag_ref, lag_sem)
    raw = [
        pltpu.make_async_copy(shot_hbm, shot_ref, raw_sem.at[0]),
        pltpu.make_async_copy(source_hbm, source_ref, raw_sem.at[1]),
        pltpu.make_async_copy(record_hbm, record_ref, raw_sem.at[2]),
    ]

    @pl.when(d == 0)
    def _():
        for load in raw:
            load.start()

    for load in load_e:
        load.start()
    load_lag.start()
    barrier = pltpu.get_barrier_semaphore()
    for other in (partner, up, down, across):
        pl.semaphore_signal(barrier, inc=1, device_id={"freq": other}, device_id_type=MESH)

    @pl.when(d > 0)
    def _():
        pl.semaphore_signal(barrier, inc=1, device_id={"depth": d - 1}, device_id_type=MESH)

    def build():
        load_lag.wait()

        def one_lag(lag, carry):
            sel[lag] = jnp.where(lag_ref[...] == lag, 1.0, 0.0).astype(BF16)
            g[lag, :, ROWS:, :] = jnp.zeros((2, ROWS, LANES), F32)
            return carry

        lax.fori_loop(0, DEPTHS, one_lag, 0)

    @pl.when(d > 0)
    def _():
        build()

    @pl.when(d == 0)
    def _():
        for load in raw:
            load.wait()
        straight = lax.broadcasted_iota(jnp.int32, (1, SHOTS), 1)
        packed = []
        for field_ref, shots in ((source_ref, shot_ref[...]), (record_ref, straight)):
            lines = field_ref[...].reshape(2 * SHOTS, POINTS)
            rows = lax.dot_general(
                route(shots), lines, (((0,), (0,)), ((), ())), preferred_element_type=F32
            )
            packed.append(rows.reshape(BATCHES, HALF, POINTS))
        inbuf[...] = jnp.concatenate(packed, axis=1).astype(BF16)

    @pl.when(d < DEPTHS - 1)
    def _():
        pl.semaphore_wait(barrier, 5)

    @pl.when(d == DEPTHS - 1)
    def _():
        pl.semaphore_wait(barrier, 4)

    def hop(b, n):
        columns = pl.ds(n * side, side)
        return pltpu.make_async_remote_copy(
            src_ref=fin.at[b, :, columns],
            dst_ref=inbuf.at[b, :, columns],
            send_sem=chain_send.at[2 * b + n],
            recv_sem=chain_recv.at[2 * b + n],
            device_id={"depth": d + 1},
            device_id_type=MESH,
        )

    def step(b, first_step=False):
        if first_step:
            load_e[0].wait()

        @pl.when(d > 0)
        def _():
            hop(b, 0).wait_recv()

        values = inbuf[b, :, sides[0]]
        first = jnp.dot(values, e_ref[0, sides[0], :], preferred_element_type=F32)
        second = jnp.dot(values, e_ref[1, sides[0], :], preferred_element_type=F32)

        @pl.when(d > 0)
        def _():
            hop(b, 1).wait_recv()

        if first_step:
            load_e[1].wait()
        values = inbuf[b, :, sides[1]]
        results = []
        for n in range(2):
            part_first = first[:, sides[n]] + jnp.dot(
                values, e_ref[0, sides[1], sides[n]], preferred_element_type=F32
            )
            part_second = second[:, sides[n]] + jnp.dot(
                values, e_ref[1, sides[1], sides[n]], preferred_element_type=F32
            )
            result = swap_parts(part_first, part_second)
            fin[b, :, sides[n]] = result.astype(BF16)

            @pl.when(d < DEPTHS - 1)
            def _():
                hop(b, n).start()

            results.append(result)
        return results

    def two_steps(p, carry, first_step=False):
        even = step(2 * p, first_step)
        odd = step(2 * p + 1)
        rows = pl.ds(pl.multiple_of(p * 2 * HALF, 2 * HALF), 2 * HALF)
        for n in range(2):
            field[0, rows, sides[n]] = jnp.concatenate(
                [even[n][:HALF], odd[n][:HALF]], axis=0
            ).astype(BF16)
            field[1, rows, sides[n]] = jnp.concatenate(
                [even[n][HALF:], odd[n][HALF:]], axis=0
            ).astype(BF16)
        return carry

    @pl.when(d > 0)
    def _():
        pl.semaphore_wait(token_sem, 1)

    @pl.when(d < DEPTHS - 1)
    def _():
        pl.semaphore_signal(token_sem, inc=1, device_id={"depth": d + 1}, device_id_type=MESH)

    def greet(k, carry):
        for peer in (f, across):
            pl.semaphore_signal(
                greet_sem, inc=1, device_id={"depth": k, "freq": peer}, device_id_type=MESH
            )
        return carry

    lax.fori_loop(0, d, greet, 0)
    two_steps(0, 0, True)
    lax.fori_loop(1, BATCHES // 2, two_steps, 0)

    mine = pl.ds(pl.multiple_of(core * ROWS, ROWS), ROWS)
    theirs = pl.ds(pl.multiple_of((1 - core) * ROWS, ROWS), ROWS)

    def to_core(t):
        return pltpu.make_async_remote_copy(
            src_ref=part.at[t, theirs, :],
            dst_ref=corein.at[t],
            send_sem=core_send.at[t],
            recv_sem=core_recv.at[t],
            device_id={"freq": partner},
            device_id_type=MESH,
        )

    factor = factor_ref[0]
    for pair_start in range(0, len(ORDER), 2):
        for t in (pair_start, pair_start + 1):
            q, r = ORDER[t]
            block = (yh + q * (1 - 2 * yh)) * 4 + (x + r) % 4
            columns = pl.ds(pl.multiple_of(block * 2 * ROWS, 2 * ROWS), 2 * ROWS)
            term = lax.dot_general(
                field[0, :, columns], field[1], (((0,), (0,)), ((), ())), preferred_element_type=F32
            )
            part[t] = (term * factor).astype(BF16)
        to_core(pair_start).start()
        to_core(pair_start + 1).start()

    @pl.when(d == 0)
    def _():
        build()

    def pair(t, rows=slice(0, ROWS)):
        own = part[t, mine, :][rows]
        return own.astype(F32) + corein[t, rows, :].astype(F32)

    def ring(src, dst, s, target):
        return pltpu.make_async_remote_copy(
            src_ref=src,
            dst_ref=dst,
            send_sem=x_send.at[s],
            recv_sem=x_recv.at[s],
            device_id={"freq": target},
            device_id_type=MESH,
        )

    low, high = slice(0, ROWS // 2), slice(ROWS // 2, ROWS)
    copies = {}
    for q in (0, 1):
        base = 6 * q
        lo, hi = pl.ds(0, ROWS // 2), pl.ds(ROWS // 2, ROWS // 2)
        copies[q] = dict(
            two_up=ring(two.at[q, lo, :], rel_up.at[q], base, up),
            two_down=ring(two.at[q, hi, :], rel_down.at[q], base + 1, down),
            one_now=ring(one.at[q, hi, :], from_down.at[q, hi, :], base + 2, up),
            one_late=ring(one.at[q, lo, :], from_down.at[q, lo, :], base + 3, up),
            three_now=ring(three.at[q, lo, :], from_up.at[q, lo, :], base + 4, down),
            three_late=ring(three.at[q, hi, :], from_up.at[q, hi, :], base + 5, down),
        )

    def far(q):
        t = ORDER.index((q, 2))
        to_core(t).wait_recv()
        two[q] = pair(t).astype(BF16)
        copies[q]["two_up"].start()
        copies[q]["two_down"].start()

    def near(q):
        t = ORDER.index((q, 1))
        to_core(t).wait_recv()
        one[q] = pair(t).astype(BF16)
        copies[q]["one_now"].start()
        t = ORDER.index((q, 3))
        to_core(t).wait_recv()
        three[q] = pair(t).astype(BF16)
        copies[q]["three_now"].start()

    def relay(q):
        copies[q]["two_up"].wait_recv()
        one[q, low, :] = (one[q, low, :].astype(F32) + rel_up[q].astype(F32)).astype(BF16)
        copies[q]["one_late"].start()
        copies[q]["two_down"].wait_recv()
        three[q, high, :] = (three[q, high, :].astype(F32) + rel_down[q].astype(F32)).astype(BF16)
        copies[q]["three_late"].start()

    def collect(q):
        t = ORDER.index((q, 0))
        to_core(t).wait_recv()
        for name in ("one_now", "three_now", "one_late", "three_late"):
            copies[q][name].wait_recv()
        return pair(t) + from_down[q].astype(F32) + from_up[q].astype(F32)

    far(1)
    near(1)
    far(0)
    relay(1)
    near(0)
    relay(0)

    def deal(q, k):
        target = (d + k) % DEPTHS
        return pltpu.make_async_remote_copy(
            src_ref=pieces.at[q, target],
            dst_ref=gath.at[q, d],
            send_sem=d_send.at[q, k],
            recv_sem=d_recv.at[q, k],
            device_id={"depth": target, "freq": across if q else f},
            device_id_type=MESH,
        )

    def arrival(q, k):
        source = (d + DEPTHS - k) % DEPTHS
        return pltpu.make_async_remote_copy(
            src_ref=pieces.at[q, source],
            dst_ref=gath.at[q, source],
            send_sem=d_send.at[q, k],
            recv_sem=d_recv.at[q, k],
            device_id={"depth": source, "freq": across if q else f},
            device_id_type=MESH,
        )

    for q in (1, 0):
        acc[...] = collect(q)
        for k in range(DEPTHS):
            pieces[q, k] = acc[PIECE * k : PIECE * (k + 1), :].astype(BF16)
        if q:
            @pl.when(d < DEPTHS - 1)
            def _():
                pl.semaphore_wait(greet_sem, 2 * (DEPTHS - 1 - d))

        def send_piece(i, carry):
            deal(q, DEPTHS // 2 + (i // 2 + i % 2) * (1 - 2 * (i % 2))).start()
            return carry

        lax.fori_loop(0, DEPTHS - 1, send_piece, 0)
        if q:
            deal(q, 0).start()
    gath[0, d] = pieces[0, d]

    for q in (1, 0):
        def take_piece(k, carry):
            arrival(q, k).wait_recv()
            return carry

        lax.fori_loop(1 - q, DEPTHS, take_piece, 0)
    for k in range(DEPTHS):
        xs[PIECE * k : PIECE * (k + 1), :] = gath[0, k].astype(F32) + gath[1, k].astype(F32)

    xb[...] = xs[...].astype(BF16)

    def stack(p, carry):
        lags = [GROUP * p + k for k in range(GROUP)]
        terms = [jnp.dot(xb[...], sel[lag], preferred_element_type=F32) for lag in lags]
        for lag, term in zip(lags, terms):
            g[lag, 0, 0:ROWS, :] = term[:, :LANES]
            g[lag, 1, 0:ROWS, :] = term[:, LANES:]
        return carry

    lax.fori_loop(0, DEPTHS // GROUP, stack, 0)
    scale = 1.0 / math.sqrt(POINTS)
    for row in range(PIECE):
        for wing in range(2):
            total = g[0, wing, pl.ds(row, DEPTHS, stride=PIECE), :]
            for lag in range(1, DEPTHS):
                total = total + g[lag, wing, pl.ds(PIECE * lag + row, DEPTHS, stride=PIECE), :]
            out_ref[row, :, LANES * wing : LANES * (wing + 1)] = total * scale

    @pl.when(d < DEPTHS - 1)
    def _():
        def drain(b, carry):
            hop(b, 0).wait_send()
            hop(b, 1).wait_send()
            return carry

        lax.fori_loop(0, BATCHES, drain, 0)

    for t in range(len(ORDER)):
        to_core(t).wait_send()
    for q in (0, 1):
        for copy in copies[q].values():
            copy.wait_send()
    for q in (1, 0):
        def drain_piece(k, carry):
            deal(q, k).wait_send()
            return carry

        lax.fori_loop(1 - q, DEPTHS, drain_piece, 0)


def migrate(extrap, source, record, shots, factor, angle_lag):
    vmem = pl.BlockSpec(memory_space=pltpu.VMEM)
    hbm = pl.BlockSpec(memory_space=pltpu.HBM)
    return pl.pallas_call(
        kernel,
        out_shape=jax.ShapeDtypeStruct((PIECE, DEPTHS, ANGLES), F32),
        in_specs=[hbm, hbm, hbm, hbm, pl.BlockSpec(memory_space=pltpu.SMEM), hbm],
        out_specs=vmem,
        scratch_shapes=[
            pltpu.VMEM((2, POINTS, POINTS), BF16),
            pltpu.VMEM((SHOTS, 2, POINTS), BF16),
            pltpu.VMEM((SHOTS, 2, POINTS), BF16),
            pltpu.VMEM((1, SHOTS), jnp.int32),
            pltpu.VMEM((POINTS, ANGLES), jnp.int32),
            pltpu.VMEM((BATCHES, 2 * HALF, POINTS), BF16),
            pltpu.VMEM((BATCHES, 2 * HALF, POINTS), BF16),
            pltpu.VMEM((2, 2 * SHOTS, POINTS), BF16),
            pltpu.VMEM((DEPTHS, POINTS, ANGLES), BF16),
            pltpu.VMEM((8, 2 * ROWS, POINTS), BF16),
            pltpu.VMEM((8, ROWS, POINTS), BF16),
            pltpu.VMEM((2, ROWS, POINTS), BF16),
            pltpu.VMEM((2, ROWS, POINTS), BF16),
            pltpu.VMEM((2, ROWS, POINTS), BF16),
            pltpu.VMEM((2, ROWS // 2, POINTS), BF16),
            pltpu.VMEM((2, ROWS // 2, POINTS), BF16),
            pltpu.VMEM((2, ROWS, POINTS), BF16),
            pltpu.VMEM((2, ROWS, POINTS), BF16),
            pltpu.VMEM((ROWS, POINTS), F32),
            pltpu.VMEM((2, DEPTHS, PIECE, POINTS), BF16),
            pltpu.VMEM((2, DEPTHS, PIECE, POINTS), BF16),
            pltpu.VMEM((ROWS, POINTS), F32),
            pltpu.VMEM((ROWS, POINTS), BF16),
            pltpu.VMEM((DEPTHS, 2, 2 * ROWS, LANES), F32),
            pltpu.SemaphoreType.DMA((2,)),
            pltpu.SemaphoreType.DMA,
            pltpu.SemaphoreType.DMA((3,)),
            pltpu.SemaphoreType.DMA((2 * BATCHES,)),
            pltpu.SemaphoreType.DMA((2 * BATCHES,)),
            pltpu.SemaphoreType.DMA((8,)),
            pltpu.SemaphoreType.DMA((8,)),
            pltpu.SemaphoreType.DMA((12,)),
            pltpu.SemaphoreType.DMA((12,)),
            pltpu.SemaphoreType.DMA((2, DEPTHS)),
            pltpu.SemaphoreType.DMA((2, DEPTHS)),
            pltpu.SemaphoreType.REGULAR,
            pltpu.SemaphoreType.REGULAR,
        ],
        compiler_params=pltpu.CompilerParams(
            collective_id=0, has_side_effects=True, vmem_limit_bytes=67043328 - 10400 * 1024
        ),
        name="migrate",
    )(extrap, source, record, shots, factor, angle_lag)


def shards(extrap, source_field, record_field, shot_of_record, freq_index, angle_lag):
    freq_count = lax.axis_size("freq")
    shots = shot_of_record.reshape(1, SHOTS)
    factor = (
        (freq_index.astype(F32) + 1.0) / (8 * freq_count) / math.sqrt(SHOTS * freq_count)
    )
    return migrate(
        extrap[0, 0], source_field[0], record_field[0], shots, factor, angle_lag
    )


def solution(mesh):
    placed = (
        P("depth", "freq", None, None, None),
        P("freq", None, None, None),
        P("freq", None, None, None),
        P(),
        P("freq"),
        P(),
    )
    return jax.shard_map(
        shards,
        mesh=mesh,
        in_specs=placed,
        out_specs=P(("freq", "depth"), None, None),
        check_vma=False,
    )
```
